32 devices in a mesh: sec: 2 (over core), gx: 4 (over z), gy: 4 (over y, x).
Axes of the slice: x: 2, y: 2, z: 4, core: 2. Of those that a mesh axis runs over, the one named last changes fastest.
Arguments:
- slide_thickness: float32 [8, 4, 128, 512], P(('sec', 'gy'), 'gx'), may hold values from 0.2 to 2
- footprint: int32 [8, 4, 128, 512], P(('sec', 'gy'), 'gx'), may hold values 0 or 1
- slide_momentum: float32 [8, 4, 128, 512], P(('sec', 'gy'), 'gx'), may hold values from -1.5 to 1.5
- bed_friction: float32 [8, 4, 128, 512], P(('sec', 'gy'), 'gx'), may hold values from 0.1 to 1
- surface: float32 [4096, 512], P(('sec', 'gy'), 'gx'), may hold values from -2 to 2
- flux_x: float32 [3, 4096, 512], P(None, ('sec', 'gy'), 'gx'), may hold values from -2 to 2
- flux_y: float32 [3, 4096, 512], P(None, ('sec', 'gy'), 'gx'), may hold values from -2 to 2
- bathy_class: int32 [4096, 512], P(('sec', 'gy'), 'gx'), may hold values from 0 to 7
- depth_table: float32 [8], replicated, may hold values from 2 to 8
Outputs:
- surface_out: float32 [4096, 512], P(('sec', 'gy'), 'gx')
- pressure_out: float32 [3, 4096, 512], P(None, ('sec', 'gy'), 'gx')
- bottom_load: float32 [8, 4, 128, 512], P(('sec', 'gy'), 'gx')
- thickness_out: float32 [512, 4096], P(('sec', 'gx', 'gy'))
- momentum_out: float32 [512, 4096], P(('sec', 'gx', 'gy'))
The draws below stay inside these ranges and needn't reach their ends.
All inputs are finite; a program needn't handle non-finite values. No bound on the sum of `footprint` on one device may be relied on, other than what follows from the above.
Results may differ from the reference program's by a relative error of at most 0.0001.
Values sent between devices are 32-bit elements; how exact they have to be, the bound alone decides.
No kernel may reach another device: no remote copies, remote signals or barrier semaphores. Data moves between devices by JAX's collectives and lax.ppermute only.
A program may use at most 128 MiB of HBM per device.

```python
import math
import jax
import jax.numpy as jnp
from jax import lax

LEVELS = 4
SWEEPS = 4
LAYERS = 3
NCLASS = 8
NX = 512
NY = 4096
BANDS = 8
W = 128
N_GX = 4


def with_ends(result, own_key, smallest, top_value):
    longest = result.shape.index(max(result.shape))
    spots = []
    for shift in (0, 1):
        where = [jax.random.randint(jax.random.fold_in(own_key, axis), (), 0, length) for axis, length in enumerate(result.shape)]
        where[longest] = (where[longest] + shift) % result.shape[longest]
        spots.append(tuple(where))
    return result.at[spots[0]].set(smallest).at[spots[1]].set(top_value)


def shard_levels(key, extent, cuts, least, high):
    loudness, own = 1.0, jax.random.fold_in(key, 6)
    for position, parts in cuts:
        draws = jnp.exp(jax.random.uniform(jax.random.fold_in(own, position), (parts,), jnp.float32, least / len(cuts), high / len(cuts)))
        loudness = loudness * jnp.repeat(draws, extent[position] // parts).reshape([-1 if axis == position else 1 for axis in range(len(extent))])
    return loudness


def noise(stream_key, shape, width, bound, cuts=(), held_as=jnp.bfloat16):
    level = shard_levels(stream_key, shape, cuts, -0.22, 0.18) if cuts else 1.0
    result = jax.random.normal(stream_key, shape, jnp.float32) * width * level
    return jnp.minimum(jnp.maximum(result, -bound), bound).astype(held_as)


def setup_inputs(seed: int = 0) -> dict:
    key_of = jax.random.split(jax.random.key(seed), 10)
    slide_thickness = jnp.clip(0.2 + 1.8 * jax.random.uniform(key_of[0], (BANDS, N_GX, W, NX), jnp.float32) ** shard_levels(key_of[0], (BANDS, N_GX, W, NX), ((0, 8), (1, 4)), -0.2, 0.2), 0.2, 2.0)
    footprint = with_ends((jax.random.randint(key_of[1], (BANDS, N_GX, W, NX), 0, 4) < 3).astype(jnp.int32), jax.random.fold_in(key_of[1], 1), 0, 1)
    slide_momentum = noise(key_of[2], (BANDS, N_GX, W, NX), 0.3, 1.5, ((0, 8), (1, 4)), jnp.float32)
    bed_friction = jnp.clip(jnp.exp(math.log(1.0) - 2.3025851 * jax.random.uniform(key_of[3], (BANDS, N_GX, W, NX), jnp.float32) ** shard_levels(key_of[3], (BANDS, N_GX, W, NX), ((0, 8), (1, 4)), -0.2, 0.2)), 0.1, 1.0)
    surface = noise(key_of[4], (NY, NX), 0.3, 2.0, ((0, 8), (1, 4)), jnp.float32)
    flux_x = noise(key_of[5], (LAYERS, NY, NX), 0.3, 2.0, ((1, 8), (2, 4)), jnp.float32)
    flux_y = noise(key_of[6], (LAYERS, NY, NX), 0.3, 2.0, ((1, 8), (2, 4)), jnp.float32)
    bathy_class = with_ends(jax.random.randint(key_of[7], (NY, NX), 0, NCLASS), jax.random.fold_in(key_of[7], 1), 0, NCLASS - 1).astype(jnp.int32)
    depth_table = jnp.clip(jnp.exp(jax.random.uniform(key_of[8], (NCLASS,), jnp.float32, math.log(2.0), math.log(8.0))), 2.0, 8.0)
    return {"slide_thickness": slide_thickness, "footprint": footprint, "slide_momentum": slide_momentum, "bed_friction": bed_friction, "surface": surface, "flux_x": flux_x, "flux_y": flux_y, "bathy_class": bathy_class, "depth_table": depth_table}


SPREAD = 0.25
GRAVITY_PUSH = 0.4
SOURCE = 2.0
SURFACE_STEP = 0.2
COURANT = 0.25
SLOPE_PULL = 0.5
LAYER_SHARE = (0.2, 0.3, 0.5)

def slide_step(thickness, moment, friction):
    speed = moment / (1.0 + jnp.abs(thickness))
    flux_mass = moment
    flux_moment = moment * speed + 0.5 * thickness * thickness

    def beside(field):
        padded = jnp.pad(field, ((0, 0), (1, 1)))
        return (padded[:, :-2], padded[:, 2:])
    thick_lo, thick_hi = beside(thickness)
    moment_lo, moment_hi = beside(moment)
    mass_lo, mass_hi = beside(flux_mass)
    carry_lo, carry_hi = beside(flux_moment)
    new_thickness = 0.5 * (thick_lo + thick_hi) - 0.5 * COURANT * (mass_hi - mass_lo)
    drag = friction * thickness * speed / jnp.sqrt(speed * speed + 1.0)
    new_moment = 0.5 * (moment_lo + moment_hi) - 0.5 * COURANT * (carry_hi - carry_lo) + COURANT * (SLOPE_PULL * thickness - drag)
    return (new_thickness, new_moment)

def diff_east(padded):
    return (padded[..., 1:-1, 2:] - padded[..., 1:-1, :-2]) * 0.5

def diff_north(padded):
    return (padded[..., 2:, 1:-1] - padded[..., :-2, 1:-1]) * 0.5

def neighbours(padded):
    return padded[..., 1:-1, 2:] + padded[..., 1:-1, :-2] + padded[..., 2:, 1:-1] + padded[..., :-2, 1:-1]

def lookup_depth(bathy_class, depth_table):
    water_depth = jnp.zeros(bathy_class.shape, jnp.float32)
    for class_index in range(depth_table.shape[0]):
        water_depth = water_depth + jnp.where(bathy_class == class_index, depth_table[class_index], 0.0)
    return water_depth

def vertical_inverse(water_depth):
    coupling = 9.0 / (water_depth * water_depth)
    horizontal = 4.0 * SPREAD
    diag_top = horizontal + 3.0 * coupling
    diag_mid = horizontal + 2.0 * coupling
    diag_low = horizontal + coupling
    square = coupling * coupling
    determinant = diag_top * (diag_mid * diag_low - square) - square * diag_low
    return jnp.stack([diag_mid * diag_low - square, coupling * diag_low, square, diag_top * diag_low, coupling * diag_top, diag_top * diag_mid - square]) / determinant

def apply_inverse(inverse, vector):
    top = inverse[0] * vector[0] + inverse[1] * vector[1] + inverse[2] * vector[2]
    mid = inverse[1] * vector[0] + inverse[3] * vector[1] + inverse[4] * vector[2]
    low = inverse[2] * vector[0] + inverse[4] * vector[1] + inverse[5] * vector[2]
    return jnp.stack([top, mid, low])

def pad_cells(field):
    widths = [(0, 0)] * (field.ndim - 2) + [(1, 1), (1, 1)]
    return jnp.pad(field, widths)

def reference(slide_thickness, footprint, slide_momentum, bed_friction, surface, flux_x, flux_y, bathy_class, depth_table):
    thickness = (slide_thickness * footprint.astype(jnp.float32)).reshape(NY, NX)
    moment = slide_momentum.reshape(NY, NX)
    friction = bed_friction.reshape(NY, NX)
    inverse = vertical_inverse(lookup_depth(bathy_class, depth_table))
    share = jnp.array(LAYER_SHARE, dtype=jnp.float32)[:, None, None]
    surface_now = surface
    flux_east = flux_x
    flux_north = flux_y
    pressure = jnp.zeros((LAYERS, NY, NX), jnp.float32)
    bottom_sum = jnp.zeros((NY, NX), jnp.float32)
    for level_index in range(LEVELS):
        new_thickness, moment = slide_step(thickness, moment, friction)
        seafloor_rise = new_thickness - thickness
        thickness = new_thickness
        padded = pad_cells(surface_now)
        flux_east = flux_east - GRAVITY_PUSH * diff_east(padded)
        flux_north = flux_north - GRAVITY_PUSH * diff_north(padded)
        source_term = -(diff_east(pad_cells(flux_east)) + diff_north(pad_cells(flux_north))) + SOURCE * share * seafloor_rise
        for sweep in range(SWEEPS):
            pressure = apply_inverse(inverse, source_term + SPREAD * neighbours(pad_cells(pressure)))
        padded_pressure = pad_cells(pressure)
        flux_east = flux_east - SPREAD * diff_east(padded_pressure)
        flux_north = flux_north - SPREAD * diff_north(padded_pressure)
        surface_now = surface_now - SURFACE_STEP * lax.optimization_barrier(jnp.sum(diff_east(pad_cells(flux_east)) + diff_north(pad_cells(flux_north)), axis=0)) + seafloor_rise
        bottom_sum = bottom_sum + pressure[2]
    bottom_load = (bottom_sum / LEVELS).reshape(BANDS, N_GX, W, NX)
    return (surface_now, pressure, bottom_load, thickness.T, moment.T)
```

```python
import functools

import jax
import jax.numpy as jnp
from jax import lax
from jax.experimental import pallas as pl
from jax.experimental.pallas import tpu as pltpu
from jax.sharding import PartitionSpec as P

LEVELS = 4
SWEEPS = 4
LAYERS = 3

GRAVITY_PUSH = 0.4
SPREAD = 0.25
SOURCE = 2.0
SURFACE_STEP = 0.2
COURANT = 0.25
SLOPE_PULL = 0.5
LAYER_SHARE = (0.2, 0.3, 0.5)

STEP = SWEEPS + 3
RIM = LEVELS * STEP
EDGE = 32
LANES = 128
TOP = 8
F32 = jnp.float32


def smem():
    return pl.BlockSpec(memory_space=pltpu.SMEM)


def vmem():
    return pl.BlockSpec(memory_space=pltpu.VMEM)


def call(kernel, scalars, inputs, outs, scratch=(), flops=10**6, moved=10**6, name=None):
    return pl.pallas_call(
        kernel,
        out_shape=[jax.ShapeDtypeStruct(s, F32) for s in outs],
        in_specs=[smem()] * len(scalars) + [vmem()] * len(inputs),
        out_specs=[vmem() for _ in outs],
        scratch_shapes=list(scratch),
        cost_estimate=pl.CostEstimate(flops=flops, bytes_accessed=moved, transcendentals=0),
        name=name,
    )(*scalars, *inputs)


def lane_of(shape):
    return lax.broadcasted_iota(jnp.int32, shape, len(shape) - 1)


def row_of(shape):
    return lax.broadcasted_iota(jnp.int32, shape, len(shape) - 2)


def pack_slide_kernel(n, tile_x, where_ref, th, fp, mo, fr, *rest):
    blocks, turned = rest[:n], rest[n]
    cells_x = th.shape[1]
    deep = tile_x + 2 * RIM
    g = where_ref[0]
    fields = (
        lambda cols: th[:, cols] * fp[:, cols].astype(F32),
        lambda cols: mo[:, cols],
        lambda cols: fr[:, cols],
    )
    for a, field in enumerate(fields):
        turned[a, :RIM, :] = jnp.zeros((RIM, LANES), F32)
        turned[a, RIM + cells_x :, :] = jnp.zeros((RIM, LANES), F32)
        for i in range(cells_x // LANES):
            turned[a, RIM + i * LANES : RIM + (i + 1) * LANES, :] = field(
                slice(i * LANES, (i + 1) * LANES)
            ).T
    for shift in range(n):
        start = pl.multiple_of(lax.rem(g + shift, n) * tile_x, 8)
        for a in range(3):
            blocks[shift][a * deep : (a + 1) * deep, :] = turned[a, pl.ds(start, deep), :]


def slide_kernel(th, fp, mo, fr, out_h, out_m, hs, ms):
    w, cells = th.shape
    lane = lane_of((8, cells))

    def body(c, carry):
        rows = pl.ds(pl.multiple_of(c * 8, 8), 8)
        h = th[rows, :] * fp[rows, :].astype(F32)
        m = mo[rows, :]
        f = fr[rows, :]

        def lo(v):
            return jnp.where(lane == 0, 0.0, pltpu.roll(v, 1, 1))

        def hi(v):
            return jnp.where(lane == cells - 1, 0.0, pltpu.roll(v, cells - 1, 1))

        for _ in range(LEVELS):
            u = m / (1.0 + jnp.abs(h))
            carry_m = m * u + 0.5 * h * h
            drag = f * h * u / jnp.sqrt(u * u + 1.0)
            m_lo, m_hi = lo(m), hi(m)
            new_h = 0.5 * (lo(h) + hi(h)) - 0.5 * COURANT * (m_hi - m_lo)
            m = (
                0.5 * (m_lo + m_hi)
                - 0.5 * COURANT * (hi(carry_m) - lo(carry_m))
                + COURANT * (SLOPE_PULL * h - drag)
            )
            h = new_h
        hs[rows, :] = h
        ms[rows, :] = m
        return carry

    lax.fori_loop(0, w // 8, body, 0)
    for i in range(cells // LANES):
        cols = slice(i * LANES, (i + 1) * LANES)
        out_h[cols, :] = hs[:, cols].T
        out_m[cols, :] = ms[:, cols].T


def pack_wave_kernel(table, eta, fx, fy, cls, low, high, wide, edge_u, v_pad):
    tile_y, tile_x = eta.shape
    count = table.shape[0]
    lane = lane_of((LANES, tile_x))
    v_pad[:, :8, :] = jnp.zeros((LAYERS, 8, tile_x), F32)
    v_pad[:, 8 + tile_y :, :] = jnp.zeros((LAYERS, 8, tile_x), F32)
    for k in range(LAYERS):
        v_pad[k, 8 : 8 + tile_y, :] = fy[k]
    last = tile_y // LANES - 1
    for i in range(tile_y // LANES):
        rows = slice(i * LANES, (i + 1) * LANES)

        def keep(a, value, turned=True):
            if i == 0:
                low[a * EDGE : (a + 1) * EDGE, :] = value[:EDGE]
            if i == last:
                high[a * EDGE : (a + 1) * EDGE, :] = value[LANES - EDGE :]
            if a < 5:
                wide[a, :, rows] = value.T
            else:
                edge_u[:, rows] = value.T[:8]

        keep(0, eta[rows, :])
        ends = jnp.zeros((LANES, tile_x), F32)
        for k in range(LAYERS):
            u = fx[k, rows, :]
            right = jnp.where(lane == tile_x - 1, 0.0, pltpu.roll(u, tile_x - 1, 1))
            left = jnp.where(lane == 0, 0.0, pltpu.roll(u, 1, 1))
            up = v_pad[k, 9 + i * LANES : 9 + (i + 1) * LANES, :]
            down = v_pad[k, 7 + i * LANES : 7 + (i + 1) * LANES, :]
            keep(1 + k, 2.0 * ((right - left) + (up - down)))
            head = u if k == 0 else pltpu.roll(u, k, 1)
            ends = jnp.where(lane == k, head, ends)
            ends = jnp.where(lane == LAYERS + k, pltpu.roll(u, LAYERS + k + 1, 1), ends)
        found = cls[rows, :]
        depth = jnp.zeros((LANES, tile_x), F32)
        for j in range(count):
            depth = jnp.where(found == j, table[j], depth)
        keep(4, depth)
        keep(5, ends)
    base = 6 * EDGE
    low[base:, :] = jnp.zeros((8, tile_x), F32)
    high[base:, :] = jnp.zeros((8, tile_x), F32)
    for k in range(LAYERS):
        low[base + k : base + k + 1, :] = fy[k, 0:1, :]
        high[base + k : base + k + 1, :] = fy[k, tile_y - 1 : tile_y, :]


def widen_wave_kernel(where_ref, wide, edge_u, low, high, from_low, from_high, out, out_u, send_a, send_b):
    g, b, nb = where_ref[0], where_ref[1], where_ref[3]
    tile_x, tile_y = wide.shape[1:]
    tiles = tile_y // LANES
    has_low = (b > 0).astype(F32)
    has_high = (b < nb - 1).astype(F32)
    row = row_of((EDGE, tile_x))
    lane = lane_of((tile_x, LANES))
    row_full = row_of((LANES, tile_x))
    base = 6 * EDGE
    gap = jnp.zeros((LANES - 2 * EDGE, tile_x), F32)
    for a in range(6):
        up = from_high[a * EDGE : (a + 1) * EDGE, :]
        down = from_low[a * EDGE : (a + 1) * EDGE, :]
        if a == 0:
            up = up * has_high
            down = down * has_low
        if 1 <= a <= LAYERS:
            v_top = high[base + a - 1 : base + a, :]
            v_bottom = low[base + a - 1 : base + a, :]
            up = up - jnp.where(row == 0, 2.0 * v_top, 0.0)
            down = down + jnp.where(row == EDGE - 1, 2.0 * v_bottom, 0.0)
        extra = jnp.concatenate([up, gap, down], axis=0).T
        if a == 5:
            for t in range(tiles):
                out_u[t] = edge_u[:, t * LANES : (t + 1) * LANES]
            out_u[tiles] = extra[:8]
            continue
        out[a, tiles] = extra
        for t in range(tiles):
            out[a, t] = wide[a, :, t * LANES : (t + 1) * LANES]
        if 1 <= a <= LAYERS:
            v_above = from_high[base + a - 1 : base + a, :] * (2.0 * has_high)
            v_below = from_low[base + a - 1 : base + a, :] * (2.0 * has_low)
            fix = jnp.where(row_full == LANES - 1, v_above, jnp.where(row_full == 0, -v_below, 0.0)).T
            out[a, tiles - 1] = out[a, tiles - 1] + jnp.where(lane == LANES - 1, fix, 0.0)
            out[a, 0] = out[a, 0] + jnp.where(lane == 0, fix, 0.0)

    def fill(send, right):
        for t in range(tiles + 1):
            for a in range(5):
                at = (t * 5 + a) * RIM
                rows = slice(tile_x - RIM, tile_x) if right else slice(0, RIM)
                send[at : at + RIM, :] = out[a, t, rows, :]
            at = (tiles + 1) * 5 * RIM + t * 4
            rows = slice(LAYERS, LAYERS + 4) if right else slice(0, 4)
            send[at : at + 4, :] = out_u[t, rows, :]

    even = lax.rem(g, 2) == 0

    @pl.when(even)
    def _():
        fill(send_a, True)
        fill(send_b, False)

    @pl.when(jnp.logical_not(even))
    def _():
        fill(send_a, False)
        fill(send_b, True)


def slide_edge_kernel(n, w, where_ref, *refs):
    blocks = refs[:n]
    low, high, head, tail = refs[n:]
    g = where_ref[0]
    rows = blocks[0].shape[0]
    part = low.shape[0]
    head[rows:, :] = jnp.zeros((head.shape[0] - rows, LANES), F32)
    tail[rows:, :] = jnp.zeros((tail.shape[0] - rows, LANES), F32)
    for shift in range(n):

        @pl.when(g == shift)
        def _():
            head[:rows, :] = blocks[shift][...]

        @pl.when(lax.rem(g + 1, n) == shift)
        def _():
            tail[:rows, :] = blocks[shift][...]

    lane = lane_of((part, LANES))
    packed_low = jnp.zeros((part, LANES), F32)
    packed_high = jnp.zeros((part, LANES), F32)
    for p in range(LANES // EDGE):
        here = (lane >= p * EDGE) & (lane < (p + 1) * EDGE)
        v = head[p * part : (p + 1) * part, :]
        turn = (p * EDGE) % LANES
        packed_low = jnp.where(here, pltpu.roll(v, turn, 1) if turn else v, packed_low)
        v = tail[p * part : (p + 1) * part, :]
        turn = (p * EDGE - (w - EDGE)) % LANES
        packed_high = jnp.where(here, pltpu.roll(v, turn, 1) if turn else v, packed_high)
    low[...] = packed_low
    high[...] = packed_high


def wave_kernel(n, w, cells_x, cells_y, where_ref, *refs):
    (wide, edge_u, got_a, got_b, slide_low, slide_high) = refs[:6]
    blocks = refs[6 : 6 + n]
    loads = refs[6 + n : 6 + 2 * n]
    fields_out = refs[6 + 2 * n]
    (eta, div, src, pa, pb, coef, corner, hs, ms, fs, qs, rise, load, stage, left, right) = refs[
        7 + 2 * n :
    ]
    g, b = where_ref[0], where_ref[1]
    tiles, tile_x = wide.shape[1] - 1, wide.shape[2]
    every = range(tiles + 1)
    tile_y = tiles * LANES
    deep = tile_x + 2 * RIM
    total = TOP + deep + TOP
    own = TOP + RIM

    even = lax.rem(g, 2) == 0

    @pl.when(even)
    def _():
        right[...] = got_a[...]
        left[...] = got_b[...]

    @pl.when(jnp.logical_not(even))
    def _():
        left[...] = got_a[...]
        right[...] = got_b[...]

    blank = jnp.zeros((TOP, LANES), F32)
    for t in every:
        for ref in (eta, hs.at[0], hs.at[1], ms.at[0], ms.at[1], qs):
            ref[t, :TOP, :] = blank
            ref[t, total - TOP :, :] = blank
        for k in range(LAYERS):
            for ref in (pa.at[k], pb.at[k]):
                ref[t, :TOP, :] = blank
                ref[t, total - TOP :, :] = blank
        for a, ref in enumerate((eta, div.at[0], div.at[1], div.at[2], corner)):
            at = (t * 5 + a) * RIM
            ref[t, own - RIM : own, :] = left[at : at + RIM, :]
            ref[t, own : own + tile_x, :] = wide[a, t]
            ref[t, own + tile_x : own + tile_x + RIM, :] = right[at : at + RIM, :]
        base = (tiles + 1) * 5 * RIM + t * 4
        end = own + tile_x
        for k in range(LAYERS):
            d = div.at[k]

            def bump(at, value):
                d[t, at : at + 1, :] = d[t, at : at + 1, :] + 2.0 * value

            bump(end - 1, right[base + k : base + k + 1, :])
            bump(end, -edge_u[t, LAYERS + k : LAYERS + k + 1, :])
            bump(own, -left[base + k : base + k + 1, :])
            bump(own - 1, edge_u[t, k : k + 1, :])

    slides = (hs.at[0], ms.at[0], fs)
    if w == LANES:
        for shift in range(n):
            q = lax.rem(g - shift + n, n)
            for a, ref in enumerate(slides):
                ref[q, TOP : TOP + deep, :] = blocks[shift][a * deep : (a + 1) * deep, :]
    else:
        per = LANES // w
        lane_d = lane_of((deep, LANES))
        for a, ref in enumerate(slides):
            for shift in range(n):
                stage[lax.rem(g - shift + n, n), :deep, :] = blocks[shift][a * deep : (a + 1) * deep, :]
            for t in range(tiles):
                v = stage[t * per, :deep, :]
                for j in range(1, per):
                    v = jnp.where(
                        lane_d < j * w, v, pltpu.roll(stage[t * per + j, :deep, :], j * w, 1)
                    )
                ref[t, TOP : TOP + deep, :] = v
    part = slide_low.shape[0]
    lane_p = lane_of((part, LANES))
    for p in range(LANES // EDGE):
        turn = (-p * EDGE) % LANES
        up = slide_high[...]
        up = pltpu.roll(up, turn, 1) if turn else up
        turn = (LANES - EDGE - p * EDGE) % LANES
        down = slide_low[...]
        down = pltpu.roll(down, turn, 1) if turn else down
        stage[0, p * part : (p + 1) * part, :] = jnp.where(
            lane_p < EDGE, up, jnp.where(lane_p >= LANES - EDGE, down, 0.0)
        )
    for a, ref in enumerate(slides):
        ref[tiles, TOP : TOP + deep, :] = stage[0, a * deep : (a + 1) * deep, :]

    lane = lane_of((8, LANES))
    row = row_of((8, LANES))

    def y_of(t):
        local = lane + t * LANES
        if t == tiles:
            local = jnp.where(lane < EDGE, local, lane - LANES)
        return local + b * tile_y

    def y_in(t):
        y = y_of(t)
        return (y >= 0) & (y < cells_y) & ((lane < EDGE) | (lane >= LANES - EDGE))

    def x_in(c):
        x = row + (c * 8 - RIM) + g * tile_x
        return (x >= 0) & (x < cells_x)

    def masked(c, t, value):
        mine = c * 8 >= RIM and c * 8 + 8 <= RIM + tile_x
        if not mine:
            value = jnp.where(x_in(c), value, 0.0)
        if t == tiles:
            value = jnp.where(y_in(t), value, 0.0)
        return value

    def coefficients(c, carry):
        at = pl.ds(pl.multiple_of(TOP + c * 8, 8), 8)
        x = row + (c * 8 - RIM) + g * tile_x
        x_ok = (x >= 0) & (x < cells_x)
        x_ends = 4.0 - (x == 0).astype(F32) - (x == cells_x - 1).astype(F32)
        for t in every:
            y = y_of(t)
            inside = x_ok & y_in(t) if t == tiles else x_ok
            depth = jnp.where(inside, corner[t, at, :], 1.0)
            k = 9.0 / (depth * depth)
            p1 = 1.0 / (1.0 + 3.0 * k)
            l1 = k * p1
            p2 = 1.0 / ((1.0 + 2.0 * k) - k * l1)
            l2 = k * p2
            p3 = 1.0 / ((1.0 + k) - k * l2)
            coef[0, t, at, :] = l1
            coef[1, t, at, :] = l2
            coef[2, t, at, :] = jnp.where(inside, SPREAD * p1, 0.0)
            coef[3, t, at, :] = jnp.where(inside, SPREAD * p2, 0.0)
            coef[4, t, at, :] = jnp.where(inside, SPREAD * p3, 0.0)
            corner[t, at, :] = x_ends - (y == 0).astype(F32) - (y == cells_y - 1).astype(F32)
        return carry

    lax.fori_loop(0, deep // 8, coefficients, 0)

    def chunks(width):
        width = min(width, RIM)
        return range((RIM - width) // 8, -(-(RIM + tile_x + width) // 8))

    def rows(ref, t, c, by=0):
        return ref[t, TOP + c * 8 + by : TOP + c * 8 + by + 8, :]

    def put(ref, t, c, value):
        ref[t, TOP + c * 8 : TOP + c * 8 + 8, :] = value

    def around(ref, c, reach):
        mid = [rows(ref, t, c) for t in every]
        fore = [pltpu.roll(v, reach, 1) for v in mid]
        back = [pltpu.roll(v, LANES - reach, 1) for v in mid]
        ring = []
        for t in every:
            west = jnp.where(lane < reach, fore[t - 1], fore[t])
            east = jnp.where(lane >= LANES - reach, back[(t + 1) % (tiles + 1)], back[t])
            ring.append((west + east) + (rows(ref, t, c, -reach) + rows(ref, t, c, reach)))
        return mid, ring

    def solve(t, c, g1, g2, g3, out):
        l1, l2 = rows(coef.at[0], t, c), rows(coef.at[1], t, c)
        g2 = g2 + l1 * g1
        g3 = g3 + l2 * g2
        x3 = rows(coef.at[4], t, c) * g3
        x2 = rows(coef.at[3], t, c) * g2 + l2 * x3
        x1 = rows(coef.at[2], t, c) * g1 + l1 * x2
        put(out.at[0], t, c, x1)
        put(out.at[1], t, c, x2)
        put(out.at[2], t, c, x3)

    for level in range(LEVELS):
        reach = (LEVELS - level) * STEP
        h_now, h_new = hs.at[level % 2], hs.at[(level + 1) % 2]
        m_now, m_new = ms.at[level % 2], ms.at[(level + 1) % 2]
        moving = level < LEVELS - 1
        if moving:
            for c in chunks(reach):
                for t in every:
                    h, m = rows(h_now, t, c), rows(m_now, t, c)
                    u = m / (1.0 + jnp.abs(h))
                    put(qs, t, c, m * u + 0.5 * h * h)
                    drag = rows(fs, t, c) * h * u * lax.rsqrt(u * u + 1.0)
                    put(m_new, t, c, COURANT * (SLOPE_PULL * h - drag))
        for c in chunks(reach - 1):
            for t in every:
                h = rows(h_now, t, c)
                m_lo, m_hi = rows(m_now, t, c, -1), rows(m_now, t, c, 1)
                h_lo, h_hi = rows(h_now, t, c, -1), rows(h_now, t, c, 1)
                fresh = 0.5 * (h_lo + h_hi) - 0.5 * COURANT * (m_hi - m_lo)
                mine = c * 8 >= RIM and c * 8 + 8 <= RIM + tile_x
                if not mine:
                    fresh = jnp.where(x_in(c), fresh, 0.0)
                put(rise, t, c, fresh - h)
                if moving:
                    q_lo, q_hi = rows(qs, t, c, -1), rows(qs, t, c, 1)
                    moved = (0.5 * (m_lo + m_hi) - 0.5 * COURANT * (q_hi - q_lo)) + rows(m_new, t, c)
                    if not mine:
                        moved = jnp.where(x_in(c), moved, 0.0)
                    put(h_new, t, c, fresh)
                    put(m_new, t, c, moved)
        for c in chunks(reach - 2):
            mid, ring = around(eta, c, 2)
            for t in every:
                push = GRAVITY_PUSH * (ring[t] - rows(corner, t, c) * mid[t])
                up = rows(rise, t, c)
                vector = []
                for k in range(LAYERS):
                    d = rows(div.at[k], t, c) - push
                    put(div.at[k], t, c, d)
                    s = (4.0 * SOURCE * LAYER_SHARE[k]) * up - d
                    put(src.at[k], t, c, s)
                    vector.append(s)
                if level == 0:
                    solve(t, c, *vector, pb)
        done = 1 if level == 0 else 0
        for sweep in range(done, SWEEPS):
            old, new = (pa, pb) if sweep % 2 == 0 else (pb, pa)
            for c in chunks(reach - 2 - sweep):
                rings = [around(old.at[k], c, 1)[1] for k in range(LAYERS)]
                for t in every:
                    solve(t, c, *(rings[k][t] + rows(src.at[k], t, c) for k in range(LAYERS)), new)
        press = pa if SWEEPS % 2 == 0 else pb
        for c in chunks(reach - STEP):
            flow = None
            for k in range(LAYERS):
                mid, ring = around(press.at[k], c, 2)
                ds = [
                    rows(div.at[k], t, c) - SPREAD * (ring[t] - rows(corner, t, c) * mid[t])
                    for t in every
                ]
                if moving:
                    for t in every:
                        put(div.at[k], t, c, ds[t])
                flow = ds if flow is None else [f + d for f, d in zip(flow, ds)]
            for t in every:
                change = rows(rise, t, c) - (0.25 * SURFACE_STEP) * flow[t]
                put(eta, t, c, rows(eta, t, c) + masked(c, t, change))
        for c in chunks(0):
            for t in range(tiles):
                bottom = rows(press.at[LAYERS - 1], t, c)
                if level > 0:
                    bottom = rows(load, t, c) + bottom
                put(load, t, c, bottom * (1.0 / LEVELS) if level == LEVELS - 1 else bottom)
    for q in range(n):
        for shift in range(n):

            @pl.when(lax.rem(g + shift, n) == q)
            def _():
                turned = load[q * w // LANES, own : own + tile_x, :].T
                loads[shift][...] = turned[q * w % LANES : q * w % LANES + w, :]

    press = pa if SWEEPS % 2 == 0 else pb
    for t in range(tiles):
        fields_out[0, t] = eta[t, own : own + tile_x, :]
        for k in range(LAYERS):
            fields_out[1 + k, t] = press[k, t, own : own + tile_x, :]


def turn_kernel(fields, eta_out, press_out):
    for i in range(fields.shape[1]):
        rows = slice(i * LANES, (i + 1) * LANES)
        eta_out[rows, :] = fields[0, i].T
        for k in range(LAYERS):
            press_out[k, rows, :] = fields[1 + k, i].T


def place_load_kernel(n, where_ref, *refs):
    parts, out = refs[:n], refs[n]
    g = where_ref[0]
    tile_x = parts[0].shape[1]
    for shift in range(n):
        col = pl.multiple_of(lax.rem(g - shift + n, n) * tile_x, LANES)
        out[:, pl.ds(col, tile_x)] = parts[shift][...]


def shards(
    slide_thickness,
    footprint,
    slide_momentum,
    bed_friction,
    surface,
    flux_x,
    flux_y,
    bathy_class,
    depth_table,
):
    th, fp, mo, fr = (v[0, 0] for v in (slide_thickness, footprint, slide_momentum, bed_friction))
    w, cells_x = th.shape
    tile_y, tile_x = surface.shape
    n = lax.axis_size("gx")
    secs, gys = lax.axis_size("sec"), lax.axis_size("gy")
    nb = secs * gys
    along = ("sec", "gy")
    g = lax.axis_index("gx")
    b = lax.axis_index(along)
    where = jnp.stack([g, b, jnp.int32(n), jnp.int32(nb)]).astype(jnp.int32)
    deep = tile_x + 2 * RIM
    tiles = tile_y // LANES + 1
    total = TOP + deep + TOP

    def padded(v):
        return v if w >= LANES else jnp.pad(v, ((0, LANES - w), (0, 0)))

    def turn(v, axis, count, by):
        return lax.ppermute(v, axis, [(i, (i + by) % count) for i in range(count)])

    blocks = call(
        functools.partial(pack_slide_kernel, n, tile_x),
        [where],
        [padded(v) for v in (th, fp, mo, fr)],
        [(3 * deep, LANES)] * n,
        [pltpu.VMEM((3, cells_x + 2 * RIM, LANES), F32)],
        name="pack_slide",
    )
    blocks = [blocks[0]] + [turn(blocks[s], "gx", n, s) for s in range(1, n)]

    edge_rows = 6 * EDGE + 8
    low, high, wide, edge_u = call(
        pack_wave_kernel,
        [depth_table],
        [surface, flux_x, flux_y, bathy_class],
        [(edge_rows, tile_x)] * 2 + [(5, tile_x, tile_y), (8, tile_y)],
        [pltpu.VMEM((LAYERS, tile_y + 16, tile_x), F32)],
        name="pack_wave",
    )
    from_low = turn(high, along, nb, 1)
    from_high = turn(low, along, nb, -1)
    halo = (tiles * (5 * RIM + 4), LANES)
    wide, edge_u, send_a, send_b = call(
        widen_wave_kernel,
        [where],
        [wide, edge_u, low, high, from_low, from_high],
        [(5, tiles, tile_x, LANES), (tiles, 8, LANES)] + [halo] * 2,
        name="widen_wave",
    )

    def swap(v, first):
        pairs = [(i, i + 1) for i in range(first, n - 1, 2)]
        return lax.ppermute(v, "gx", pairs + [(j, i) for i, j in pairs])

    got_a = swap(send_a, 0)
    got_b = swap(send_b, 1)

    part = -(-3 * deep // (8 * (LANES // EDGE))) * 8
    rows = part * (LANES // EDGE)
    slide_low, slide_high = call(
        functools.partial(slide_edge_kernel, n, w),
        [where],
        blocks,
        [(part, LANES)] * 2,
        [pltpu.VMEM((rows, LANES), F32)] * 2,
        name="slide_edge",
    )
    slide_from_low = turn(slide_high, along, nb, 1)
    slide_from_high = turn(slide_low, along, nb, -1)

    last_h, last_m = call(
        slide_kernel,
        [],
        [padded(v) for v in (th, fp, mo, fr)],
        [(cells_x, LANES)] * 2,
        [pltpu.VMEM((LANES, cells_x), F32)] * 2,
        name="slide",
    )
    devices = secs * n * gys
    own_rows = cells_x // devices
    both = jnp.stack([v[:, :w].reshape(devices, own_rows, w) for v in (last_h, last_m)], axis=1)
    both = lax.all_to_all(both, ("sec", "gx", "gy"), split_axis=0, concat_axis=0, tiled=True)
    both = both.reshape(secs, n, gys, 2, own_rows, w)
    both = jnp.transpose(both, (3, 4, 0, 2, 1, 5)).reshape(2, own_rows, -1)

    one = (tiles, total, LANES)
    stage_count = 1 if w == LANES else n
    results = call(
        functools.partial(wave_kernel, n, w, cells_x, nb * tile_y),
        [where],
        [wide, edge_u, got_a, got_b, slide_from_low, slide_from_high, *blocks],
        [(w, tile_x)] * n + [(4, tiles - 1, tile_x, LANES)],
        [
            pltpu.VMEM(shape, F32)
            for shape in (
                one,
                (LAYERS, *one),
                (LAYERS, *one),
                (LAYERS, *one),
                (LAYERS, *one),
                (5, *one),
                one,
                (2, *one),
                (2, *one),
                one,
                one,
                one,
                (tiles - 1, total, LANES),
                (stage_count, rows, LANES),
                halo,
                halo,
            )
        ],
        flops=10**9,
        moved=10**7,
        name="wave",
    )
    loads, fields = results[:n], results[n]
    parts = [loads[0]] + [turn(loads[s], "gx", n, s) for s in range(1, n)]
    surface_out, pressure_out = call(
        turn_kernel, [], [fields], [(tile_y, tile_x), (LAYERS, tile_y, tile_x)], name="turn"
    )
    (bottom,) = call(
        functools.partial(place_load_kernel, n), [where], parts, [(w, cells_x)], name="place_load"
    )
    return (surface_out, pressure_out, bottom[None, None], both[0], both[1])


def solution(mesh):
    strip = P(("sec", "gy"), "gx", None, None)
    tile = P(("sec", "gy"), "gx")
    layered = P(None, ("sec", "gy"), "gx")
    return jax.shard_map(
        shards,
        mesh=mesh,
        in_specs=(strip, strip, strip, strip, tile, layered, layered, tile, P()),
        out_specs=(
            tile,
            layered,
            strip,
            P(("sec", "gx", "gy"), None),
            P(("sec", "gx", "gy"), None),
        ),
        check_vma=False,
    )
```

```python
import functools

import jax
import jax.numpy as jnp
from jax import lax
from jax.experimental import pallas as pl
from jax.experimental.pallas import tpu as pltpu
from jax.sharding import PartitionSpec as P


LEVELS = 4
SWEEPS = 4
LAYERS = 3

GRAVITY_PUSH = 0.4
SPREAD = 0.25
SOURCE = 2.0
SURFACE_STEP = 0.2
COURANT = 0.25
SLOPE_PULL = 0.5
LAYER_SHARE = (0.2, 0.3, 0.5)

STEP = SWEEPS + 3
RIM = LEVELS * STEP
TRIM = STEP + 1
EDGE = 32
LANES = 128
GROUP = 2
TOP = 8
F32 = jnp.float32


def smem():
    return pl.BlockSpec(memory_space=pltpu.SMEM)


def vmem():
    return pl.BlockSpec(memory_space=pltpu.VMEM)


def fetching(kernel, lead, count):
    def body(*refs):
        scalars, inputs, rest = refs[:lead], refs[lead : lead + count], refs[lead + count :]
        held, sems = rest[-count - 1 : -1], rest[-1]
        copies = [
            pltpu.make_async_copy(src, dst, sems.at[i])
            for i, (src, dst) in enumerate(zip(inputs, held))
        ]
        for copy in copies:
            copy.start()
        for copy in copies:
            copy.wait()
        kernel(*scalars, *held, *rest[: -count - 1])

    return body


def call(kernel, scalars, inputs, outs, scratch=(), flops=10**6, moved=10**6, room=12, fetch=False):
    in_spec, scratch = vmem(), list(scratch)
    if fetch:
        in_spec = pl.BlockSpec(memory_space=pltpu.HBM)
        kernel = fetching(kernel, len(scalars), len(inputs))
        scratch += [pltpu.VMEM(v.shape, v.dtype) for v in inputs]
        scratch.append(pltpu.SemaphoreType.DMA((len(inputs),)))
    return pl.pallas_call(
        kernel,
        out_shape=[jax.ShapeDtypeStruct(s, F32) for s in outs],
        in_specs=[smem()] * len(scalars) + [in_spec] * len(inputs),
        out_specs=[vmem() for _ in outs],
        scratch_shapes=scratch,
        cost_estimate=pl.CostEstimate(flops=flops, bytes_accessed=moved, transcendentals=0),
        compiler_params=pltpu.CompilerParams(vmem_limit_bytes=room << 20),
    )(*scalars, *inputs)


def strip_place():
    return lax.axis_index("gx")


def band_place():
    return lax.axis_index("sec") * lax.axis_size("gy") + lax.axis_index("gy")


def receiver(g, shift, n):
    return lax.bitwise_xor(g, shift) if n & (n - 1) == 0 else lax.rem(g + shift, n)


def sender(g, shift, n):
    return lax.bitwise_xor(g, shift) if n & (n - 1) == 0 else lax.rem(g - shift + n, n)


def lane_of(shape):
    return lax.broadcasted_iota(jnp.int32, shape, len(shape) - 1)


def row_of(shape):
    return lax.broadcasted_iota(jnp.int32, shape, len(shape) - 2)


def pack_slide_kernel(n, tile_x, th, fp, mo, fr, *rest):
    blocks, turned = rest[:n], rest[n]
    cells_x = th.shape[1]
    deep = tile_x + 2 * RIM
    g = strip_place()
    fields = (
        lambda cols: th[:, cols] * fp[:, cols].astype(F32),
        lambda cols: mo[:, cols],
        lambda cols: fr[:, cols],
    )
    for a, field in enumerate(fields):
        turned[a, :RIM, :] = jnp.zeros((RIM, LANES), F32)
        turned[a, RIM + cells_x :, :] = jnp.zeros((RIM, LANES), F32)
        for i in range(cells_x // LANES):
            turned[a, RIM + i * LANES : RIM + (i + 1) * LANES, :] = field(
                slice(i * LANES, (i + 1) * LANES)
            ).T
    for shift in range(n):
        start = pl.multiple_of(receiver(g, shift, n) * tile_x, 8)
        for a in range(3):
            cut = TRIM if a == 2 else 0
            size = deep - 2 * cut
            blocks[shift][a * deep : a * deep + size, :] = turned[a, pl.ds(start + cut, size), :]


def slide_kernel(th, fp, mo, fr, out, hs, ms, qs, fs):
    devices, _, own_rows, _ = out.shape
    cells = th.shape[1]
    zero = jnp.zeros((8, LANES), F32)
    for ref in (hs.at[0], hs.at[1], ms.at[0], ms.at[1], qs):
        ref[:8, :] = zero
        ref[8 + cells :, :] = zero
    for i in range(cells // LANES):
        cols = slice(i * LANES, (i + 1) * LANES)
        at = slice(8 + i * LANES, 8 + (i + 1) * LANES)
        hs[0, at, :] = (th[:, cols] * fp[:, cols].astype(F32)).T
        ms[0, at, :] = mo[:, cols].T
        fs[at, :] = fr[:, cols].T
    rows = 32 if cells % 32 == 0 else 8
    for level in range(LEVELS):
        h_now, h_new = hs.at[level % 2], hs.at[(level + 1) % 2]
        m_now, m_new = ms.at[level % 2], ms.at[(level + 1) % 2]
        for c in range(cells // rows):
            at = slice(8 + c * rows, 8 + (c + 1) * rows)
            h, m = h_now[at, :], m_now[at, :]
            u = m / (1.0 + jnp.abs(h))
            qs[at, :] = m * u + 0.5 * h * h
            m_new[at, :] = COURANT * (SLOPE_PULL * h - fs[at, :] * h * u * lax.rsqrt(u * u + 1.0))
        for c in range(cells // rows):
            at = slice(8 + c * rows, 8 + (c + 1) * rows)
            lo = slice(7 + c * rows, 7 + (c + 1) * rows)
            hi = slice(9 + c * rows, 9 + (c + 1) * rows)
            m_lo, m_hi = m_now[lo, :], m_now[hi, :]
            h_new[at, :] = 0.5 * (h_now[lo, :] + h_now[hi, :]) - 0.5 * COURANT * (m_hi - m_lo)
            m_new[at, :] = (
                0.5 * (m_lo + m_hi) - 0.5 * COURANT * (qs[hi, :] - qs[lo, :])
            ) + m_new[at, :]
    for d in range(devices):
        at = slice(8 + d * own_rows, 8 + (d + 1) * own_rows)
        out[d, 0] = hs[LEVELS % 2, at, :]
        out[d, 1] = ms[LEVELS % 2, at, :]


def place_slide_kernel(secs, n, gys, both, out_h, out_m):
    w = both.shape[3]
    for s in range(secs):
        for g in range(n):
            for y in range(gys):
                at = ((s * gys + y) * n + g) * w
                src = (s * n + g) * gys + y
                out_h[:, at : at + w] = both[src, 0]
                out_m[:, at : at + w] = both[src, 1]


def pack_wave_kernel(table, eta, fx, fy, cls, low, high, wide, edge_u, v_pad):
    tile_y, tile_x = eta.shape
    count = table.shape[0]
    lane = lane_of((LANES, tile_x))
    v_pad[:, :8, :] = jnp.zeros((LAYERS, 8, tile_x), F32)
    v_pad[:, 8 + tile_y :, :] = jnp.zeros((LAYERS, 8, tile_x), F32)
    for k in range(LAYERS):
        v_pad[k, 8 : 8 + tile_y, :] = fy[k]
    last = tile_y // LANES - 1
    for i in range(tile_y // LANES):
        rows = slice(i * LANES, (i + 1) * LANES)

        def keep(a, value):
            if i == 0:
                low[a * EDGE : (a + 1) * EDGE, :] = value[:EDGE]
            if i == last:
                high[a * EDGE : (a + 1) * EDGE, :] = value[LANES - EDGE :]
            if a < 5:
                wide[a, :, rows] = value.T
            else:
                edge_u[:, rows] = value.T[:8]

        keep(0, eta[rows, :])
        ends = jnp.zeros((LANES, tile_x), F32)
        for k in range(LAYERS):
            u = fx[k, rows, :]
            right = jnp.where(lane == tile_x - 1, 0.0, pltpu.roll(u, tile_x - 1, 1))
            left = jnp.where(lane == 0, 0.0, pltpu.roll(u, 1, 1))
            up = v_pad[k, 9 + i * LANES : 9 + (i + 1) * LANES, :]
            down = v_pad[k, 7 + i * LANES : 7 + (i + 1) * LANES, :]
            keep(1 + k, 2.0 * ((right - left) + (up - down)))
            head = u if k == 0 else pltpu.roll(u, k, 1)
            ends = jnp.where(lane == k, head, ends)
            ends = jnp.where(lane == LAYERS + k, pltpu.roll(u, LAYERS + k + 1, 1), ends)
        found = cls[rows, :]
        depth = jnp.zeros((LANES, tile_x), F32)
        for j in range(count):
            depth = jnp.where(found == j, table[j], depth)
        keep(4, depth)
        keep(5, ends)
    base = 6 * EDGE
    low[base:, :] = jnp.zeros((8, tile_x), F32)
    high[base:, :] = jnp.zeros((8, tile_x), F32)
    for k in range(LAYERS):
        low[base + k : base + k + 1, :] = fy[k, 0:1, :]
        high[base + k : base + k + 1, :] = fy[k, tile_y - 1 : tile_y, :]


def widen_wave_kernel(nb, wide, edge_u, low, high, from_low, from_high, out, out_u, send_a, send_b):
    g, b = strip_place(), band_place()
    tile_x, tile_y = wide.shape[1:]
    tiles = tile_y // LANES
    has_low = (b > 0).astype(F32)
    has_high = (b < nb - 1).astype(F32)
    row = row_of((EDGE, tile_x))
    lane = lane_of((tile_x, LANES))
    row_full = row_of((LANES, tile_x))
    base = 6 * EDGE
    gap = jnp.zeros((LANES - 2 * EDGE, tile_x), F32)
    for a in range(6):
        up = from_high[a * EDGE : (a + 1) * EDGE, :]
        down = from_low[a * EDGE : (a + 1) * EDGE, :]
        if a == 0:
            up = up * has_high
            down = down * has_low
        if 1 <= a <= LAYERS:
            v_top = high[base + a - 1 : base + a, :]
            v_bottom = low[base + a - 1 : base + a, :]
            up = up - jnp.where(row == 0, 2.0 * v_top, 0.0)
            down = down + jnp.where(row == EDGE - 1, 2.0 * v_bottom, 0.0)
        extra = jnp.concatenate([up, gap, down], axis=0).T
        if a == 5:
            for t in range(tiles):
                out_u[t] = edge_u[:, t * LANES : (t + 1) * LANES]
            out_u[tiles] = extra[:8]
            continue
        out[a, tiles] = extra
        for t in range(tiles):
            out[a, t] = wide[a, :, t * LANES : (t + 1) * LANES]
        if 1 <= a <= LAYERS:
            v_above = from_high[base + a - 1 : base + a, :] * (2.0 * has_high)
            v_below = from_low[base + a - 1 : base + a, :] * (2.0 * has_low)
            fix = jnp.where(row_full == LANES - 1, v_above, jnp.where(row_full == 0, -v_below, 0.0)).T
            out[a, tiles - 1] = out[a, tiles - 1] + jnp.where(lane == LANES - 1, fix, 0.0)
            out[a, 0] = out[a, 0] + jnp.where(lane == 0, fix, 0.0)

    def fill(send, right):
        for t in range(tiles + 1):
            for a in range(5):
                at = (t * 5 + a) * RIM
                rows = slice(tile_x - RIM, tile_x) if right else slice(0, RIM)
                send[at : at + RIM, :] = out[a, t, rows, :]
            at = (tiles + 1) * 5 * RIM + t * 4
            rows = slice(LAYERS, LAYERS + 4) if right else slice(0, 4)
            send[at : at + 4, :] = out_u[t, rows, :]

    even = lax.rem(g, 2) == 0

    @pl.when(even)
    def _():
        fill(send_a, True)
        fill(send_b, False)

    @pl.when(jnp.logical_not(even))
    def _():
        fill(send_a, False)
        fill(send_b, True)


def slide_edge_kernel(n, w, *refs):
    blocks = refs[:n]
    low, high, head, tail = refs[n:]
    g = strip_place()
    rows = blocks[0].shape[0]
    part = low.shape[0]
    head[rows:, :] = jnp.zeros((head.shape[0] - rows, LANES), F32)
    tail[rows:, :] = jnp.zeros((tail.shape[0] - rows, LANES), F32)
    for shift in range(n):

        @pl.when(sender(g, shift, n) == 0)
        def _():
            head[:rows, :] = blocks[shift][...]

        @pl.when(sender(g, shift, n) == n - 1)
        def _():
            tail[:rows, :] = blocks[shift][...]

    lane = lane_of((part, LANES))
    packed_low = jnp.zeros((part, LANES), F32)
    packed_high = jnp.zeros((part, LANES), F32)
    for p in range(LANES // EDGE):
        here = (lane >= p * EDGE) & (lane < (p + 1) * EDGE)
        v = head[p * part : (p + 1) * part, :]
        turn = (p * EDGE) % LANES
        packed_low = jnp.where(here, pltpu.roll(v, turn, 1) if turn else v, packed_low)
        v = tail[p * part : (p + 1) * part, :]
        turn = (p * EDGE - (w - EDGE)) % LANES
        packed_high = jnp.where(here, pltpu.roll(v, turn, 1) if turn else v, packed_high)
    low[...] = packed_low
    high[...] = packed_high


def wave_kernel(n, w, cells_x, cells_y, *refs):
    (wide, edge_u, got_a, got_b, slide_low, slide_high) = refs[:6]
    blocks = refs[6 : 6 + n]
    loads = refs[6 + n : 6 + 2 * n]
    fields_out = refs[6 + 2 * n]
    (eta, div, src, pa, pb, coef, corner, hs, ms, fs, qs, rise, load, bottoms, stage, left, right) = refs[
        7 + 2 * n :
    ]
    g, b = strip_place(), band_place()
    tiles, tile_x = wide.shape[1] - 1, wide.shape[2]
    every = range(tiles + 1)
    tile_y = tiles * LANES
    deep = tile_x + 2 * RIM
    total = TOP + deep + TOP
    own = TOP + RIM

    even = lax.rem(g, 2) == 0

    @pl.when(even)
    def _():
        right[...] = got_a[...]
        left[...] = got_b[...]

    @pl.when(jnp.logical_not(even))
    def _():
        left[...] = got_a[...]
        right[...] = got_b[...]

    blank = jnp.zeros((TOP, LANES), F32)
    for t in every:
        for ref in (eta, hs.at[0], hs.at[1], ms.at[0], ms.at[1], qs):
            ref[t, :TOP, :] = blank
            ref[t, total - TOP :, :] = blank
        for k in range(LAYERS):
            for ref in (pa.at[k], pb.at[k]):
                ref[t, :TOP, :] = blank
                ref[t, total - TOP :, :] = blank
        for a, ref in enumerate((eta, div.at[0], div.at[1], div.at[2], corner)):
            at = (t * 5 + a) * RIM
            ref[t, own - RIM : own, :] = left[at : at + RIM, :]
            ref[t, own : own + tile_x, :] = wide[a, t]
            ref[t, own + tile_x : own + tile_x + RIM, :] = right[at : at + RIM, :]
        base = (tiles + 1) * 5 * RIM + t * 4
        end = own + tile_x
        for k in range(LAYERS):
            d = div.at[k]

            def bump(at, value):
                d[t, at : at + 1, :] = d[t, at : at + 1, :] + 2.0 * value

            bump(end - 1, right[base + k : base + k + 1, :])
            bump(end, -edge_u[t, LAYERS + k : LAYERS + k + 1, :])
            bump(own, -left[base + k : base + k + 1, :])
            bump(own - 1, edge_u[t, k : k + 1, :])

    slides = (
        (hs.at[0], TOP, 0, deep),
        (ms.at[0], TOP, deep, deep),
        (fs, TOP + TRIM, 2 * deep, deep - 2 * TRIM),
    )
    for t in every:
        fs[t, TOP : TOP + TRIM, :] = jnp.zeros((TRIM, LANES), F32)
        fs[t, TOP + deep - TRIM : TOP + deep, :] = jnp.zeros((TRIM, LANES), F32)
    if w == LANES:
        for shift in range(n):
            q = sender(g, shift, n)
            for ref, to, at, size in slides:
                ref[q, to : to + size, :] = blocks[shift][at : at + size, :]
    else:
        per = LANES // w
        for ref, to, at, size in slides:
            lane_d = lane_of((size, LANES))
            for shift in range(n):
                stage[sender(g, shift, n), :size, :] = blocks[shift][at : at + size, :]
            for t in range(tiles):
                v = stage[t * per, :size, :]
                for j in range(1, per):
                    v = jnp.where(
                        lane_d < j * w, v, pltpu.roll(stage[t * per + j, :size, :], j * w, 1)
                    )
                ref[t, to : to + size, :] = v
    part = slide_low.shape[0]
    lane_p = lane_of((part, LANES))
    for p in range(LANES // EDGE):
        turn = (-p * EDGE) % LANES
        up = slide_high[...]
        up = pltpu.roll(up, turn, 1) if turn else up
        turn = (LANES - EDGE - p * EDGE) % LANES
        down = slide_low[...]
        down = pltpu.roll(down, turn, 1) if turn else down
        stage[0, p * part : (p + 1) * part, :] = jnp.where(
            lane_p < EDGE, up, jnp.where(lane_p >= LANES - EDGE, down, 0.0)
        )
    for ref, to, at, size in slides:
        ref[tiles, to : to + size, :] = stage[0, at : at + size, :]

    lane = lane_of((8, LANES))
    row = row_of((8, LANES))

    def y_of(t, lane):
        local = lane + t * LANES
        if t == tiles:
            local = jnp.where(lane < EDGE, local, lane - LANES)
        return local + b * tile_y

    def y_in(t, lane):
        y = y_of(t, lane)
        return (y >= 0) & (y < cells_y) & ((lane < EDGE) | (lane >= LANES - EDGE))

    def x_masked(c, value):
        if c[0] * 8 >= RIM and c[0] * 8 + c[1] <= RIM + tile_x:
            return value
        x = row_of((c[1], LANES)) + (c[0] * 8 - RIM) + g * tile_x
        return jnp.where((x >= 0) & (x < cells_x), value, 0.0)

    def masked(c, t, value):
        value = x_masked(c, value)
        if t == tiles:
            value = jnp.where(y_in(t, lane_of((c[1], LANES))), value, 0.0)
        return value

    def coefficients(c, carry):
        at = pl.ds(pl.multiple_of(TOP + c * 8, 8), 8)
        x = row + (c * 8 - RIM) + g * tile_x
        x_ok = (x >= 0) & (x < cells_x)
        x_ends = 4.0 - (x == 0).astype(F32) - (x == cells_x - 1).astype(F32)
        for t in every:
            y = y_of(t, lane)
            inside = x_ok & y_in(t, lane) if t == tiles else x_ok
            depth = jnp.where(inside, corner[t, at, :], 1.0)
            k = 9.0 / (depth * depth)
            p1 = 1.0 / (1.0 + 3.0 * k)
            l1 = k * p1
            p2 = 1.0 / ((1.0 + 2.0 * k) - k * l1)
            l2 = k * p2
            p3 = 1.0 / ((1.0 + k) - k * l2)
            coef[0, t, at, :] = l1
            coef[1, t, at, :] = l2
            coef[2, t, at, :] = jnp.where(inside, SPREAD * p1, 0.0)
            coef[3, t, at, :] = jnp.where(inside, SPREAD * p2, 0.0)
            coef[4, t, at, :] = jnp.where(inside, SPREAD * p3, 0.0)
            corner[t, at, :] = x_ends - (y == 0).astype(F32) - (y == cells_y - 1).astype(F32)
        return carry

    lax.fori_loop(0, deep // 8, coefficients, 0)

    def chunks(width):
        width = min(width, RIM)
        first, stop = (RIM - width) // 8, -(-(RIM + tile_x + width) // 8)
        return [(c, min(GROUP, stop - c) * 8) for c in range(first, stop, GROUP)]

    def rows(ref, t, c, by=0):
        at = TOP + c[0] * 8 + by
        return ref[t, at : at + c[1], :]

    def put(ref, t, c, value):
        at = TOP + c[0] * 8
        ref[t, at : at + c[1], :] = value

    def around(ref, c, reach):
        lane_c = lane_of((c[1], LANES))
        mids, fores, backs = {}, {}, {}

        def mid(t):
            t = t % (tiles + 1)
            if t not in mids:
                mids[t] = rows(ref, t, c)
            return mids[t]

        def rolled(cache, t, by):
            t = t % (tiles + 1)
            if t not in cache:
                cache[t] = pltpu.roll(mid(t), by, 1)
            return cache[t]

        def ring(t):
            fore = functools.partial(rolled, fores, by=reach)
            back = functools.partial(rolled, backs, by=LANES - reach)
            west = jnp.where(lane_c < reach, fore(t - 1), fore(t))
            east = jnp.where(lane_c >= LANES - reach, back(t + 1), back(t))
            return (west + east) + (rows(ref, t, c, -reach) + rows(ref, t, c, reach))

        return mid, ring

    def solve(t, c, g1, g2, g3, out):
        l1, l2 = rows(coef.at[0], t, c), rows(coef.at[1], t, c)
        g2 = g2 + l1 * g1
        g3 = g3 + l2 * g2
        x3 = rows(coef.at[4], t, c) * g3
        x2 = rows(coef.at[3], t, c) * g2 + l2 * x3
        x1 = rows(coef.at[2], t, c) * g1 + l1 * x2
        put(out.at[0], t, c, x1)
        put(out.at[1], t, c, x2)
        put(out.at[2], t, c, x3)

    for level in range(LEVELS):
        reach = (LEVELS - level) * STEP
        h_now, h_new = hs.at[level % 2], hs.at[(level + 1) % 2]
        m_now, m_new = ms.at[level % 2], ms.at[(level + 1) % 2]
        moving = level < LEVELS - 1
        if moving:
            for c in chunks(reach):
                for t in every:
                    h, m = rows(h_now, t, c), rows(m_now, t, c)
                    u = m / (1.0 + jnp.abs(h))
                    put(qs, t, c, m * u + 0.5 * h * h)
                    drag = rows(fs, t, c) * h * u * lax.rsqrt(u * u + 1.0)
                    put(m_new, t, c, COURANT * (SLOPE_PULL * h - drag))
        for c in chunks(reach - 1):
            for t in every:
                h = rows(h_now, t, c)
                m_lo, m_hi = rows(m_now, t, c, -1), rows(m_now, t, c, 1)
                h_lo, h_hi = rows(h_now, t, c, -1), rows(h_now, t, c, 1)
                fresh = 0.5 * (h_lo + h_hi) - 0.5 * COURANT * (m_hi - m_lo)
                fresh = x_masked(c, fresh)
                put(rise, t, c, fresh - h)
                if moving:
                    q_lo, q_hi = rows(qs, t, c, -1), rows(qs, t, c, 1)
                    moved = (0.5 * (m_lo + m_hi) - 0.5 * COURANT * (q_hi - q_lo)) + rows(m_new, t, c)
                    put(h_new, t, c, fresh)
                    put(m_new, t, c, x_masked(c, moved))
        for c in chunks(reach - 2):
            mid, ring = around(eta, c, 2)
            for t in every:
                push = GRAVITY_PUSH * (ring(t) - rows(corner, t, c) * mid(t))
                up = rows(rise, t, c)
                vector = []
                for k in range(LAYERS):
                    d = rows(div.at[k], t, c) - push
                    put(div.at[k], t, c, d)
                    s = (4.0 * SOURCE * LAYER_SHARE[k]) * up - d
                    put(src.at[k], t, c, s)
                    vector.append(s)
                if level == 0:
                    solve(t, c, *vector, pb)

        def sweep(old, new, width):
            for c in chunks(width):
                rings = [around(old.at[k], c, 1)[1] for k in range(LAYERS)]
                for t in every:
                    solve(t, c, *(rings[k](t) + rows(src.at[k], t, c) for k in range(LAYERS)), new)

        pairs = SWEEPS // 2
        if level == 0:
            sweep(pb, pa, reach - 3)
            pairs -= 1

        def two(i, carry):
            sweep(pa, pb, reach - 2)
            sweep(pb, pa, reach - 3)
            return carry

        lax.fori_loop(0, pairs, two, 0)
        press = pa
        for c in chunks(reach - STEP):
            stencils = [around(press.at[k], c, 2) for k in range(LAYERS)]
            for t in every:
                flow = None
                for k in range(LAYERS):
                    mid, ring = stencils[k]
                    d = rows(div.at[k], t, c) - SPREAD * (ring(t) - rows(corner, t, c) * mid(t))
                    if moving:
                        put(div.at[k], t, c, d)
                    flow = d if flow is None else flow + d
                change = rows(rise, t, c) - (0.25 * SURFACE_STEP) * flow
                put(eta, t, c, rows(eta, t, c) + masked(c, t, change))
        for c in chunks(0):
            for t in range(tiles):
                bottom = rows(press.at[LAYERS - 1], t, c)
                if level > 0:
                    bottom = rows(load, t, c) + bottom
                put(load, t, c, bottom * (1.0 / LEVELS) if level == LEVELS - 1 else bottom)
    for q in range(n):
        turned = load[q * w // LANES, own : own + tile_x, :].T
        bottoms[q] = turned[q * w % LANES : q * w % LANES + w, :]
    for shift in range(n):
        loads[shift][...] = bottoms[receiver(g, shift, n)]
    for t in range(tiles):
        fields_out[0, t] = eta[t, own : own + tile_x, :]
        for k in range(LAYERS):
            fields_out[1 + k, t] = pa[k, t, own : own + tile_x, :]


def turn_kernel(fields, eta_out, press_out):
    for i in range(fields.shape[1]):
        rows = slice(i * LANES, (i + 1) * LANES)
        eta_out[rows, :] = fields[0, i].T
        for k in range(LAYERS):
            press_out[k, rows, :] = fields[1 + k, i].T


def place_load_kernel(n, *refs):
    parts, out = refs[:n], refs[n]
    g = strip_place()
    tile_x = parts[0].shape[1]
    for shift in range(n):
        col = pl.multiple_of(sender(g, shift, n) * tile_x, LANES)
        out[:, pl.ds(col, tile_x)] = parts[shift][...]


def shards(
    slide_thickness,
    footprint,
    slide_momentum,
    bed_friction,
    surface,
    flux_x,
    flux_y,
    bathy_class,
    depth_table,
):
    th, fp, mo, fr = (v[0, 0] for v in (slide_thickness, footprint, slide_momentum, bed_friction))
    w, cells_x = th.shape
    tile_y, tile_x = surface.shape
    n = lax.axis_size("gx")
    secs, gys = lax.axis_size("sec"), lax.axis_size("gy")
    nb = secs * gys
    along = ("sec", "gy")
    deep = tile_x + 2 * RIM
    tiles = tile_y // LANES + 1
    total = TOP + deep + TOP

    def padded(v):
        return v if w >= LANES else jnp.pad(v, ((0, LANES - w), (0, 0)))

    def turn(v, axis, count, by):
        return lax.ppermute(v, axis, [(i, (i + by) % count) for i in range(count)])

    def across(v, shift):
        pairs = [(i, i ^ shift if n & (n - 1) == 0 else (i + shift) % n) for i in range(n)]
        return lax.ppermute(v, "gx", pairs)

    strips = [padded(v) for v in (th, fp, mo, fr)]
    block_rows = 3 * deep - 2 * TRIM
    blocks = call(
        functools.partial(pack_slide_kernel, n, tile_x),
        [],
        strips,
        [(block_rows, LANES)] * n,
        [pltpu.VMEM((3, cells_x + 2 * RIM, LANES), F32)],
        room=63,
        fetch=True,
    )
    blocks = [blocks[0]] + [across(blocks[s], s) for s in range(1, n)]

    edge_rows = 6 * EDGE + 8
    low, high, wide, edge_u = call(
        pack_wave_kernel,
        [depth_table],
        [surface, flux_x, flux_y, bathy_class],
        [(edge_rows, tile_x)] * 2 + [(5, tile_x, tile_y), (8, tile_y)],
        [pltpu.VMEM((LAYERS, tile_y + 16, tile_x), F32)],
        room=63,
        fetch=True,
    )
    from_low = turn(high, along, nb, 1)
    from_high = turn(low, along, nb, -1)
    halo = (tiles * (5 * RIM + 4), LANES)
    wide, edge_u, send_a, send_b = call(
        functools.partial(widen_wave_kernel, nb),
        [],
        [wide, edge_u, low, high, from_low, from_high],
        [(5, tiles, tile_x, LANES), (tiles, 8, LANES)] + [halo] * 2,
    )

    def swap(v, first):
        pairs = [(i, i + 1) for i in range(first, n - 1, 2)]
        return lax.ppermute(v, "gx", pairs + [(j, i) for i, j in pairs])

    got_a = swap(send_a, 0)
    got_b = swap(send_b, 1)

    part = -(-block_rows // (8 * (LANES // EDGE))) * 8
    rows = part * (LANES // EDGE)
    slide_low, slide_high = call(
        functools.partial(slide_edge_kernel, n, w),
        [],
        blocks,
        [(part, LANES)] * 2,
        [pltpu.VMEM((rows, LANES), F32)] * 2,
    )
    slide_from_low = turn(slide_high, along, nb, 1)
    slide_from_high = turn(slide_low, along, nb, -1)

    devices = secs * n * gys
    own_rows = cells_x // devices
    state = pltpu.VMEM((2, cells_x + 16, LANES), F32)
    (both,) = call(
        slide_kernel,
        [],
        strips,
        [(devices, 2, own_rows, LANES)],
        [state, state] + [pltpu.VMEM((cells_x + 16, LANES), F32)] * 2,
        room=63,
        fetch=True,
    )
    both = lax.all_to_all(
        both[..., :w], ("sec", "gx", "gy"), split_axis=0, concat_axis=0, tiled=True
    )

    one = (tiles, total, LANES)
    stage_count = 1 if w == LANES else n
    results = call(
        functools.partial(wave_kernel, n, w, cells_x, nb * tile_y),
        [],
        [wide, edge_u, got_a, got_b, slide_from_low, slide_from_high, *blocks],
        [(w, tile_x)] * n + [(4, tiles - 1, tile_x, LANES)],
        [
            pltpu.VMEM(shape, F32)
            for shape in (
                one,
                (LAYERS, *one),
                (LAYERS, *one),
                (LAYERS, *one),
                (LAYERS, *one),
                (5, *one),
                one,
                (2, *one),
                (2, *one),
                one,
                one,
                one,
                (tiles - 1, total, LANES),
                (n, w, tile_x),
                (stage_count, rows, LANES),
                halo,
                halo,
            )
        ],
        flops=10**9,
        moved=10**7,
        room=30,
    )
    loads, fields = results[:n], results[n]
    parts = [loads[0]] + [across(loads[s], s) for s in range(1, n)]
    surface_out, pressure_out = call(
        turn_kernel, [], [fields], [(tile_y, tile_x), (LAYERS, tile_y, tile_x)]
    )
    if w % LANES == 0:
        last_h, last_m = call(
            functools.partial(place_slide_kernel, secs, n, gys),
            [],
            [both],
            [(own_rows, devices * w)] * 2,
        )
    else:
        both = both.reshape(secs, n, gys, 2, own_rows, w)
        last_h, last_m = jnp.transpose(both, (3, 4, 0, 2, 1, 5)).reshape(2, own_rows, -1)
    parts, last_h, last_m, surface_out = lax.optimization_barrier((parts, last_h, last_m, surface_out))
    (bottom,) = call(functools.partial(place_load_kernel, n), [], parts, [(w, cells_x)])
    return (surface_out, pressure_out, bottom[None, None], last_h, last_m)


def solution(mesh):
    strip = P(("sec", "gy"), "gx", None, None)
    tile = P(("sec", "gy"), "gx")
    layered = P(None, ("sec", "gy"), "gx")
    return jax.shard_map(
        shards,
        mesh=mesh,
        in_specs=(strip, strip, strip, strip, tile, layered, layered, tile, P()),
        out_specs=(
            tile,
            layered,
            strip,
            P(("sec", "gx", "gy"), None),
            P(("sec", "gx", "gy"), None),
        ),
        check_vma=False,
    )
```

```python
import functools

import jax
import jax.numpy as jnp
from jax import lax
from jax.experimental import pallas as pl
from jax.experimental.pallas import tpu as pltpu
from jax.sharding import PartitionSpec as P


LEVELS = 4
SWEEPS = 4
LAYERS = 3

GRAVITY_PUSH = 0.4
SPREAD = 0.25
SOURCE = 2.0
SURFACE_STEP = 0.2
COURANT = 0.25
SLOPE_PULL = 0.5
LAYER_SHARE = (0.2, 0.3, 0.5)

STEP = SWEEPS + 3
RIM = LEVELS * STEP
TRIM = STEP + 1
EDGE = 32
LANES = 128
GROUP = 2
TOP = 8
F32 = jnp.float32


def smem():
    return pl.BlockSpec(memory_space=pltpu.SMEM)


def vmem():
    return pl.BlockSpec(memory_space=pltpu.VMEM)


def fetching(kernel, lead, count):
    def body(*refs):
        scalars, inputs, rest = refs[:lead], refs[lead : lead + count], refs[lead + count :]
        held, sems = rest[-count - 1 : -1], rest[-1]
        copies = [
            pltpu.make_async_copy(src, dst, sems.at[i])
            for i, (src, dst) in enumerate(zip(inputs, held))
        ]
        for copy in copies:
            copy.start()
        for copy in copies:
            copy.wait()
        kernel(*scalars, *held, *rest[: -count - 1])

    return body


def call(kernel, scalars, inputs, outs, scratch=(), flops=10**6, moved=10**6, room=12, fetch=False):
    in_spec, scratch = vmem(), list(scratch)
    if fetch:
        in_spec = pl.BlockSpec(memory_space=pltpu.HBM)
        kernel = fetching(kernel, len(scalars), len(inputs))
        scratch += [pltpu.VMEM(v.shape, v.dtype) for v in inputs]
        scratch.append(pltpu.SemaphoreType.DMA((len(inputs),)))
    return pl.pallas_call(
        kernel,
        out_shape=[jax.ShapeDtypeStruct(s, F32) for s in outs],
        in_specs=[smem()] * len(scalars) + [in_spec] * len(inputs),
        out_specs=[vmem() for _ in outs],
        scratch_shapes=scratch,
        cost_estimate=pl.CostEstimate(flops=flops, bytes_accessed=moved, transcendentals=0),
        compiler_params=pltpu.CompilerParams(vmem_limit_bytes=room << 20),
    )(*scalars, *inputs)


def strip_place():
    return lax.axis_index("gx")


def band_place():
    return lax.axis_index("sec") * lax.axis_size("gy") + lax.axis_index("gy")


def receiver(g, shift, n):
    return lax.bitwise_xor(g, shift) if n & (n - 1) == 0 else lax.rem(g + shift, n)


def sender(g, shift, n):
    return lax.bitwise_xor(g, shift) if n & (n - 1) == 0 else lax.rem(g - shift + n, n)


def lane_of(shape):
    return lax.broadcasted_iota(jnp.int32, shape, len(shape) - 1)


def row_of(shape):
    return lax.broadcasted_iota(jnp.int32, shape, len(shape) - 2)


def halo_layout(tiles):
    places, at = {}, 0
    for t in range(tiles + 1):
        for a in range(5):
            size = RIM if a == 0 else RIM - 2
            if t == tiles and a in (2, 4):
                places[t, a] = places[t, a - 1]
                continue
            places[t, a] = (at, size)
            at += size
        places[t, "u"] = (at, 4)
        at += 4
    return places, -(-at // 8) * 8


def pack_slide_kernel(n, tile_x, th, fp, mo, fr, *rest):
    blocks, turned = rest[:n], rest[n]
    cells_x = th.shape[1]
    deep = tile_x + 2 * RIM
    g = strip_place()
    fields = (
        lambda cols: th[:, cols] * fp[:, cols].astype(F32),
        lambda cols: mo[:, cols],
        lambda cols: fr[:, cols],
    )
    for a, field in enumerate(fields):
        turned[a, :RIM, :] = jnp.zeros((RIM, LANES), F32)
        turned[a, RIM + cells_x :, :] = jnp.zeros((RIM, LANES), F32)
        for i in range(cells_x // LANES):
            turned[a, RIM + i * LANES : RIM + (i + 1) * LANES, :] = field(
                slice(i * LANES, (i + 1) * LANES)
            ).T
    for shift in range(n):
        start = pl.multiple_of(receiver(g, shift, n) * tile_x, 8)
        for a in range(3):
            cut = TRIM if a == 2 else 0
            size = deep - 2 * cut
            blocks[shift][a * deep : a * deep + size, :] = turned[a, pl.ds(start + cut, size), :]


def slide_kernel(th, fp, mo, fr, out, hs, ms, qs, fs):
    devices, _, own_rows, _ = out.shape
    cells = th.shape[1]
    zero = jnp.zeros((8, LANES), F32)
    for ref in (hs.at[0], hs.at[1], ms.at[0], ms.at[1], qs):
        ref[:8, :] = zero
        ref[8 + cells :, :] = zero
    for i in range(cells // LANES):
        cols = slice(i * LANES, (i + 1) * LANES)
        at = slice(8 + i * LANES, 8 + (i + 1) * LANES)
        hs[0, at, :] = (th[:, cols] * fp[:, cols].astype(F32)).T
        ms[0, at, :] = mo[:, cols].T
        fs[at, :] = fr[:, cols].T
    rows = 32 if cells % 32 == 0 else 8
    for level in range(LEVELS):
        h_now, h_new = hs.at[level % 2], hs.at[(level + 1) % 2]
        m_now, m_new = ms.at[level % 2], ms.at[(level + 1) % 2]
        for c in range(cells // rows):
            at = slice(8 + c * rows, 8 + (c + 1) * rows)
            h, m = h_now[at, :], m_now[at, :]
            u = m / (1.0 + jnp.abs(h))
            qs[at, :] = m * u + 0.5 * h * h
            m_new[at, :] = COURANT * (SLOPE_PULL * h - fs[at, :] * h * u * lax.rsqrt(u * u + 1.0))
        for c in range(cells // rows):
            at = slice(8 + c * rows, 8 + (c + 1) * rows)
            lo = slice(7 + c * rows, 7 + (c + 1) * rows)
            hi = slice(9 + c * rows, 9 + (c + 1) * rows)
            m_lo, m_hi = m_now[lo, :], m_now[hi, :]
            h_new[at, :] = 0.5 * (h_now[lo, :] + h_now[hi, :]) - 0.5 * COURANT * (m_hi - m_lo)
            m_new[at, :] = (
                0.5 * (m_lo + m_hi) - 0.5 * COURANT * (qs[hi, :] - qs[lo, :])
            ) + m_new[at, :]
    for d in range(devices):
        at = slice(8 + d * own_rows, 8 + (d + 1) * own_rows)
        out[d, 0] = hs[LEVELS % 2, at, :]
        out[d, 1] = ms[LEVELS % 2, at, :]


def place_slide_kernel(secs, n, gys, both, out_h, out_m):
    w = both.shape[3]
    for s in range(secs):
        for g in range(n):
            for y in range(gys):
                at = ((s * gys + y) * n + g) * w
                src = (s * n + g) * gys + y
                out_h[:, at : at + w] = both[src, 0]
                out_m[:, at : at + w] = both[src, 1]


def pack_wave_kernel(table, eta, fx, fy, cls, low, high, wide, edge_u, v_pad):
    tile_y, tile_x = eta.shape
    count = table.shape[0]
    lane = lane_of((LANES, tile_x))
    v_pad[:, :8, :] = jnp.zeros((LAYERS, 8, tile_x), F32)
    v_pad[:, 8 + tile_y :, :] = jnp.zeros((LAYERS, 8, tile_x), F32)
    for k in range(LAYERS):
        v_pad[k, 8 : 8 + tile_y, :] = fy[k]
    last = tile_y // LANES - 1
    for i in range(tile_y // LANES):
        rows = slice(i * LANES, (i + 1) * LANES)

        def keep(a, value):
            if i == 0:
                low[a * EDGE : (a + 1) * EDGE, :] = value[:EDGE]
            if i == last:
                high[a * EDGE : (a + 1) * EDGE, :] = value[LANES - EDGE :]
            if a < 5:
                wide[a, :, rows] = value.T
            else:
                edge_u[:, rows] = value.T[:8]

        keep(0, eta[rows, :])
        ends = jnp.zeros((LANES, tile_x), F32)
        for k in range(LAYERS):
            u = fx[k, rows, :]
            right = jnp.where(lane == tile_x - 1, 0.0, pltpu.roll(u, tile_x - 1, 1))
            left = jnp.where(lane == 0, 0.0, pltpu.roll(u, 1, 1))
            up = v_pad[k, 9 + i * LANES : 9 + (i + 1) * LANES, :]
            down = v_pad[k, 7 + i * LANES : 7 + (i + 1) * LANES, :]
            keep(1 + k, 2.0 * ((right - left) + (up - down)))
            head = u if k == 0 else pltpu.roll(u, k, 1)
            ends = jnp.where(lane == k, head, ends)
            ends = jnp.where(lane == LAYERS + k, pltpu.roll(u, LAYERS + k + 1, 1), ends)
        found = cls[rows, :]
        depth = jnp.zeros((LANES, tile_x), F32)
        for j in range(count):
            depth = jnp.where(found == j, table[j], depth)
        keep(4, depth)
        keep(5, ends)
    base = 6 * EDGE
    low[base:, :] = jnp.zeros((8, tile_x), F32)
    high[base:, :] = jnp.zeros((8, tile_x), F32)
    for k in range(LAYERS):
        low[base + k : base + k + 1, :] = fy[k, 0:1, :]
        high[base + k : base + k + 1, :] = fy[k, tile_y - 1 : tile_y, :]


def widen_wave_kernel(nb, wide, edge_u, low, high, from_low, from_high, out, out_u, send_a, send_b):
    g, b = strip_place(), band_place()
    tile_x, tile_y = wide.shape[1:]
    tiles = tile_y // LANES
    has_low = (b > 0).astype(F32)
    has_high = (b < nb - 1).astype(F32)
    row = row_of((EDGE, tile_x))
    lane = lane_of((tile_x, LANES))
    row_full = row_of((LANES, tile_x))
    base = 6 * EDGE
    gap = jnp.zeros((LANES - 2 * EDGE, tile_x), F32)
    for a in range(6):
        up = from_high[a * EDGE : (a + 1) * EDGE, :]
        down = from_low[a * EDGE : (a + 1) * EDGE, :]
        if a == 0:
            up = up * has_high
            down = down * has_low
        if 1 <= a <= LAYERS:
            v_top = high[base + a - 1 : base + a, :]
            v_bottom = low[base + a - 1 : base + a, :]
            up = up - jnp.where(row == 0, 2.0 * v_top, 0.0)
            down = down + jnp.where(row == EDGE - 1, 2.0 * v_bottom, 0.0)
        extra = jnp.concatenate([up, gap, down], axis=0).T
        if a == 5:
            for t in range(tiles):
                out_u[t] = edge_u[:, t * LANES : (t + 1) * LANES]
            out_u[tiles] = extra[:8]
            continue
        out[a, tiles] = extra
        for t in range(tiles):
            out[a, t] = wide[a, :, t * LANES : (t + 1) * LANES]
        if 1 <= a <= LAYERS:
            v_above = from_high[base + a - 1 : base + a, :] * (2.0 * has_high)
            v_below = from_low[base + a - 1 : base + a, :] * (2.0 * has_low)
            fix = jnp.where(row_full == LANES - 1, v_above, jnp.where(row_full == 0, -v_below, 0.0)).T
            out[a, tiles - 1] = out[a, tiles - 1] + jnp.where(lane == LANES - 1, fix, 0.0)
            out[a, 0] = out[a, 0] + jnp.where(lane == 0, fix, 0.0)

    places, length = halo_layout(tiles)

    def fill(send, right):
        send[length - 8 :, :] = jnp.zeros((8, LANES), F32)
        for t in range(tiles + 1):
            for a in range(5):
                at, size = places[t, a]
                rows = slice(tile_x - size, tile_x) if right else slice(0, size)
                value = out[a, t, rows, :]
                if t == tiles and a in (2, 4):
                    middle = (lane_of(value.shape) >= EDGE) & (lane_of(value.shape) < LANES - EDGE)
                    value = jnp.where(middle, pltpu.roll(value, LANES // 2, 1), out[a - 1, t, rows, :])
                elif t == tiles and a in (1, 3):
                    continue
                send[at : at + size, :] = value
            at, size = places[t, "u"]
            rows = slice(LAYERS, LAYERS + 4) if right else slice(0, 4)
            send[at : at + size, :] = out_u[t, rows, :]

    even = lax.rem(g, 2) == 0

    @pl.when(even)
    def _():
        fill(send_a, True)
        fill(send_b, False)

    @pl.when(jnp.logical_not(even))
    def _():
        fill(send_a, False)
        fill(send_b, True)


def slide_edge_kernel(n, w, *refs):
    blocks = refs[:n]
    low, high, head, tail = refs[n:]
    g = strip_place()
    rows = blocks[0].shape[0]
    part = low.shape[0]
    head[rows:, :] = jnp.zeros((head.shape[0] - rows, LANES), F32)
    tail[rows:, :] = jnp.zeros((tail.shape[0] - rows, LANES), F32)
    for shift in range(n):

        @pl.when(sender(g, shift, n) == 0)
        def _():
            head[:rows, :] = blocks[shift][...]

        @pl.when(sender(g, shift, n) == n - 1)
        def _():
            tail[:rows, :] = blocks[shift][...]

    lane = lane_of((part, LANES))
    packed_low = jnp.zeros((part, LANES), F32)
    packed_high = jnp.zeros((part, LANES), F32)
    for p in range(LANES // EDGE):
        here = (lane >= p * EDGE) & (lane < (p + 1) * EDGE)
        v = head[p * part : (p + 1) * part, :]
        turn = (p * EDGE) % LANES
        packed_low = jnp.where(here, pltpu.roll(v, turn, 1) if turn else v, packed_low)
        v = tail[p * part : (p + 1) * part, :]
        turn = (p * EDGE - (w - EDGE)) % LANES
        packed_high = jnp.where(here, pltpu.roll(v, turn, 1) if turn else v, packed_high)
    low[...] = packed_low
    high[...] = packed_high


def wave_kernel(n, w, cells_x, cells_y, *refs):
    (wide, edge_u, got_a, got_b, slide_low, slide_high) = refs[:6]
    blocks = refs[6 : 6 + n]
    loads = refs[6 + n : 6 + 2 * n]
    fields_out = refs[6 + 2 * n]
    (eta, div, src, pa, pb, coef, corner, hs, ms, fs, qs, rise, load, bottoms, stage, left, right) = refs[
        7 + 2 * n :
    ]
    g, b = strip_place(), band_place()
    tiles, tile_x = wide.shape[1] - 1, wide.shape[2]
    every = range(tiles + 1)
    tile_y = tiles * LANES
    deep = tile_x + 2 * RIM
    total = TOP + deep + TOP
    own = TOP + RIM

    even = lax.rem(g, 2) == 0

    @pl.when(even)
    def _():
        right[...] = got_a[...]
        left[...] = got_b[...]

    @pl.when(jnp.logical_not(even))
    def _():
        left[...] = got_a[...]
        right[...] = got_b[...]

    places, _ = halo_layout(tiles)
    blank = jnp.zeros((TOP, LANES), F32)
    for t in every:
        for ref in (eta, hs.at[0], hs.at[1], ms.at[0], ms.at[1], qs):
            ref[t, :TOP, :] = blank
            ref[t, total - TOP :, :] = blank
        for k in range(LAYERS):
            for ref in (pa.at[k], pb.at[k]):
                ref[t, :TOP, :] = blank
                ref[t, total - TOP :, :] = blank
        for a, ref in enumerate((eta, div.at[0], div.at[1], div.at[2], corner)):
            at, size = places[t, a]
            before, after = left[at : at + size, :], right[at : at + size, :]
            if t == tiles and a in (2, 4):
                before = pltpu.roll(before, LANES // 2, 1)
                after = pltpu.roll(after, LANES // 2, 1)
            if size < RIM:
                ref[t, TOP : TOP + 8, :] = jnp.ones((8, LANES), F32)
                ref[t, TOP + deep - 8 : TOP + deep, :] = jnp.ones((8, LANES), F32)
            ref[t, own - size : own, :] = before
            ref[t, own : own + tile_x, :] = wide[a, t]
            ref[t, own + tile_x : own + tile_x + size, :] = after
        base = places[t, "u"][0]
        end = own + tile_x
        for k in range(LAYERS):
            d = div.at[k]

            def bump(at, value):
                d[t, at : at + 1, :] = d[t, at : at + 1, :] + 2.0 * value

            bump(end - 1, right[base + k : base + k + 1, :])
            bump(end, -edge_u[t, LAYERS + k : LAYERS + k + 1, :])
            bump(own, -left[base + k : base + k + 1, :])
            bump(own - 1, edge_u[t, k : k + 1, :])

    slides = (
        (hs.at[0], TOP, 0, deep),
        (ms.at[0], TOP, deep, deep),
        (fs, TOP + TRIM, 2 * deep, deep - 2 * TRIM),
    )
    for t in every:
        fs[t, TOP : TOP + TRIM, :] = jnp.zeros((TRIM, LANES), F32)
        fs[t, TOP + deep - TRIM : TOP + deep, :] = jnp.zeros((TRIM, LANES), F32)
    if w == LANES:
        for shift in range(n):
            q = sender(g, shift, n)
            for ref, to, at, size in slides:
                ref[q, to : to + size, :] = blocks[shift][at : at + size, :]
    else:
        per = LANES // w
        for ref, to, at, size in slides:
            lane_d = lane_of((size, LANES))
            for shift in range(n):
                stage[sender(g, shift, n), :size, :] = blocks[shift][at : at + size, :]
            for t in range(tiles):
                v = stage[t * per, :size, :]
                for j in range(1, per):
                    v = jnp.where(
                        lane_d < j * w, v, pltpu.roll(stage[t * per + j, :size, :], j * w, 1)
                    )
                ref[t, to : to + size, :] = v
    part = slide_low.shape[0]
    lane_p = lane_of((part, LANES))
    for p in range(LANES // EDGE):
        turn = (-p * EDGE) % LANES
        up = slide_high[...]
        up = pltpu.roll(up, turn, 1) if turn else up
        turn = (LANES - EDGE - p * EDGE) % LANES
        down = slide_low[...]
        down = pltpu.roll(down, turn, 1) if turn else down
        stage[0, p * part : (p + 1) * part, :] = jnp.where(
            lane_p < EDGE, up, jnp.where(lane_p >= LANES - EDGE, down, 0.0)
        )
    for ref, to, at, size in slides:
        ref[tiles, to : to + size, :] = stage[0, at : at + size, :]

    lane = lane_of((8, LANES))
    row = row_of((8, LANES))

    def y_of(t, lane):
        local = lane + t * LANES
        if t == tiles:
            local = jnp.where(lane < EDGE, local, lane - LANES)
        return local + b * tile_y

    def y_in(t, lane):
        y = y_of(t, lane)
        return (y >= 0) & (y < cells_y) & ((lane < EDGE) | (lane >= LANES - EDGE))

    def x_masked(c, value):
        if c[0] * 8 >= RIM and c[0] * 8 + c[1] <= RIM + tile_x:
            return value
        x = row_of((c[1], LANES)) + (c[0] * 8 - RIM) + g * tile_x
        return jnp.where((x >= 0) & (x < cells_x), value, 0.0)

    def masked(c, t, value):
        value = x_masked(c, value)
        if t == tiles:
            value = jnp.where(y_in(t, lane_of((c[1], LANES))), value, 0.0)
        return value

    def coefficients(c, carry):
        at = pl.ds(pl.multiple_of(TOP + c * 8, 8), 8)
        x = row + (c * 8 - RIM) + g * tile_x
        x_ok = (x >= 0) & (x < cells_x)
        x_ends = 4.0 - (x == 0).astype(F32) - (x == cells_x - 1).astype(F32)
        for t in every:
            y = y_of(t, lane)
            inside = x_ok & y_in(t, lane) if t == tiles else x_ok
            depth = jnp.where(inside, corner[t, at, :], 1.0)
            k = 9.0 / (depth * depth)
            p1 = 1.0 / (1.0 + 3.0 * k)
            l1 = k * p1
            p2 = 1.0 / ((1.0 + 2.0 * k) - k * l1)
            l2 = k * p2
            p3 = 1.0 / ((1.0 + k) - k * l2)
            coef[0, t, at, :] = l1
            coef[1, t, at, :] = l2
            coef[2, t, at, :] = jnp.where(inside, SPREAD * p1, 0.0)
            coef[3, t, at, :] = jnp.where(inside, SPREAD * p2, 0.0)
            coef[4, t, at, :] = jnp.where(inside, SPREAD * p3, 0.0)
            corner[t, at, :] = x_ends - (y == 0).astype(F32) - (y == cells_y - 1).astype(F32)
        return carry

    lax.fori_loop(0, deep // 8, coefficients, 0)

    def chunks(width):
        width = min(width, RIM)
        first, stop = (RIM - width) // 8, -(-(RIM + tile_x + width) // 8)
        return [(c, min(GROUP, stop - c) * 8) for c in range(first, stop, GROUP)]

    def rows(ref, t, c, by=0):
        at = TOP + c[0] * 8 + by
        return ref[t, at : at + c[1], :]

    def put(ref, t, c, value):
        at = TOP + c[0] * 8
        ref[t, at : at + c[1], :] = value

    def around(ref, c, reach):
        lane_c = lane_of((c[1], LANES))
        mids, fores, backs = {}, {}, {}

        def mid(t):
            t = t % (tiles + 1)
            if t not in mids:
                mids[t] = rows(ref, t, c)
            return mids[t]

        def rolled(cache, t, by):
            t = t % (tiles + 1)
            if t not in cache:
                cache[t] = pltpu.roll(mid(t), by, 1)
            return cache[t]

        def ring(t):
            fore = functools.partial(rolled, fores, by=reach)
            back = functools.partial(rolled, backs, by=LANES - reach)
            west = jnp.where(lane_c < reach, fore(t - 1), fore(t))
            east = jnp.where(lane_c >= LANES - reach, back(t + 1), back(t))
            return (west + east) + (rows(ref, t, c, -reach) + rows(ref, t, c, reach))

        return mid, ring

    def solve(t, c, g1, g2, g3, out):
        l1, l2 = rows(coef.at[0], t, c), rows(coef.at[1], t, c)
        g2 = g2 + l1 * g1
        g3 = g3 + l2 * g2
        x3 = rows(coef.at[4], t, c) * g3
        x2 = rows(coef.at[3], t, c) * g2 + l2 * x3
        x1 = rows(coef.at[2], t, c) * g1 + l1 * x2
        put(out.at[0], t, c, x1)
        put(out.at[1], t, c, x2)
        put(out.at[2], t, c, x3)

    for level in range(LEVELS):
        reach = (LEVELS - level) * STEP
        h_now, h_new = hs.at[level % 2], hs.at[(level + 1) % 2]
        m_now, m_new = ms.at[level % 2], ms.at[(level + 1) % 2]
        moving = level < LEVELS - 1
        if moving:
            for c in chunks(reach):
                for t in every:
                    h, m = rows(h_now, t, c), rows(m_now, t, c)
                    u = m / (1.0 + jnp.abs(h))
                    put(qs, t, c, m * u + 0.5 * h * h)
                    drag = rows(fs, t, c) * h * u * lax.rsqrt(u * u + 1.0)
                    put(m_new, t, c, COURANT * (SLOPE_PULL * h - drag))
        for c in chunks(reach - 1):
            for t in every:
                h = rows(h_now, t, c)
                m_lo, m_hi = rows(m_now, t, c, -1), rows(m_now, t, c, 1)
                h_lo, h_hi = rows(h_now, t, c, -1), rows(h_now, t, c, 1)
                fresh = 0.5 * (h_lo + h_hi) - 0.5 * COURANT * (m_hi - m_lo)
                fresh = x_masked(c, fresh)
                put(rise, t, c, fresh - h)
                if moving:
                    q_lo, q_hi = rows(qs, t, c, -1), rows(qs, t, c, 1)
                    moved = (0.5 * (m_lo + m_hi) - 0.5 * COURANT * (q_hi - q_lo)) + rows(m_new, t, c)
                    put(h_new, t, c, fresh)
                    put(m_new, t, c, x_masked(c, moved))
        for c in chunks(reach - 2):
            mid, ring = around(eta, c, 2)
            for t in every:
                push = GRAVITY_PUSH * (ring(t) - rows(corner, t, c) * mid(t))
                up = rows(rise, t, c)
                vector = []
                for k in range(LAYERS):
                    d = rows(div.at[k], t, c) - push
                    put(div.at[k], t, c, d)
                    s = (4.0 * SOURCE * LAYER_SHARE[k]) * up - d
                    put(src.at[k], t, c, s)
                    vector.append(s)
                if level == 0:
                    solve(t, c, *vector, pb)

        def sweep(old, new, width):
            for c in chunks(width):
                rings = [around(old.at[k], c, 1)[1] for k in range(LAYERS)]
                for t in every:
                    solve(t, c, *(rings[k](t) + rows(src.at[k], t, c) for k in range(LAYERS)), new)

        pairs = SWEEPS // 2
        if level == 0:
            sweep(pb, pa, reach - 3)
            pairs -= 1

        def two(i, carry):
            sweep(pa, pb, reach - 2)
            sweep(pb, pa, reach - 3)
            return carry

        lax.fori_loop(0, pairs, two, 0)
        press = pa
        for c in chunks(reach - STEP):
            stencils = [around(press.at[k], c, 2) for k in range(LAYERS)]
            for t in every:
                flow = None
                for k in range(LAYERS):
                    mid, ring = stencils[k]
                    d = rows(div.at[k], t, c) - SPREAD * (ring(t) - rows(corner, t, c) * mid(t))
                    if moving:
                        put(div.at[k], t, c, d)
                    flow = d if flow is None else flow + d
                change = rows(rise, t, c) - (0.25 * SURFACE_STEP) * flow
                put(eta, t, c, rows(eta, t, c) + masked(c, t, change))
        for c in chunks(0):
            for t in range(tiles):
                bottom = rows(press.at[LAYERS - 1], t, c)
                if level > 0:
                    bottom = rows(load, t, c) + bottom
                put(load, t, c, bottom * (1.0 / LEVELS) if level == LEVELS - 1 else bottom)
    for q in range(n):
        turned = load[q * w // LANES, own : own + tile_x, :].T
        bottoms[q] = turned[q * w % LANES : q * w % LANES + w, :]
    for shift in range(n):
        loads[shift][...] = bottoms[receiver(g, shift, n)]
    for t in range(tiles):
        fields_out[0, t] = eta[t, own : own + tile_x, :]
        for k in range(LAYERS):
            fields_out[1 + k, t] = pa[k, t, own : own + tile_x, :]


def turn_kernel(fields, eta_out, press_out):
    for i in range(fields.shape[1]):
        rows = slice(i * LANES, (i + 1) * LANES)
        eta_out[rows, :] = fields[0, i].T
        for k in range(LAYERS):
            press_out[k, rows, :] = fields[1 + k, i].T


def place_load_kernel(n, *refs):
    parts, out = refs[:n], refs[n]
    g = strip_place()
    tile_x = parts[0].shape[1]
    for shift in range(n):
        col = pl.multiple_of(sender(g, shift, n) * tile_x, LANES)
        out[:, pl.ds(col, tile_x)] = parts[shift][...]


def shards(
    slide_thickness,
    footprint,
    slide_momentum,
    bed_friction,
    surface,
    flux_x,
    flux_y,
    bathy_class,
    depth_table,
):
    th, fp, mo, fr = (v[0, 0] for v in (slide_thickness, footprint, slide_momentum, bed_friction))
    w, cells_x = th.shape
    tile_y, tile_x = surface.shape
    n = lax.axis_size("gx")
    secs, gys = lax.axis_size("sec"), lax.axis_size("gy")
    nb = secs * gys
    along = ("sec", "gy")
    deep = tile_x + 2 * RIM
    tiles = tile_y // LANES + 1
    total = TOP + deep + TOP

    def padded(v):
        return v if w >= LANES else jnp.pad(v, ((0, LANES - w), (0, 0)))

    def turn(v, axis, count, by):
        return lax.ppermute(v, axis, [(i, (i + by) % count) for i in range(count)])

    def across(v, shift):
        pairs = [(i, i ^ shift if n & (n - 1) == 0 else (i + shift) % n) for i in range(n)]
        return lax.ppermute(v, "gx", pairs)

    strips = [padded(v) for v in (th, fp, mo, fr)]
    block_rows = 3 * deep - 2 * TRIM
    blocks = call(
        functools.partial(pack_slide_kernel, n, tile_x),
        [],
        strips,
        [(block_rows, LANES)] * n,
        [pltpu.VMEM((3, cells_x + 2 * RIM, LANES), F32)],
        room=63,
        fetch=True,
    )
    blocks = [blocks[0]] + [across(blocks[s], s) for s in range(1, n)]

    edge_rows = 6 * EDGE + 8
    low, high, wide, edge_u = call(
        pack_wave_kernel,
        [depth_table],
        [surface, flux_x, flux_y, bathy_class],
        [(edge_rows, tile_x)] * 2 + [(5, tile_x, tile_y), (8, tile_y)],
        [pltpu.VMEM((LAYERS, tile_y + 16, tile_x), F32)],
        fetch=True,
    )
    from_low = turn(high, along, nb, 1)
    from_high = turn(low, along, nb, -1)
    halo = (halo_layout(tiles - 1)[1], LANES)
    wide, edge_u, send_a, send_b = call(
        functools.partial(widen_wave_kernel, nb),
        [],
        [wide, edge_u, low, high, from_low, from_high],
        [(5, tiles, tile_x, LANES), (tiles, 8, LANES)] + [halo] * 2,
    )

    def swap(v, first):
        pairs = [(i, i + 1) for i in range(first, n - 1, 2)]
        return lax.ppermute(v, "gx", pairs + [(j, i) for i, j in pairs])

    got_a = swap(send_a, 0)
    got_b = swap(send_b, 1)

    part = -(-block_rows // (8 * (LANES // EDGE))) * 8
    rows = part * (LANES // EDGE)
    slide_low, slide_high = call(
        functools.partial(slide_edge_kernel, n, w),
        [],
        blocks,
        [(part, LANES)] * 2,
        [pltpu.VMEM((rows, LANES), F32)] * 2,
    )
    slide_from_low = turn(slide_high, along, nb, 1)
    slide_from_high = turn(slide_low, along, nb, -1)

    devices = secs * n * gys
    own_rows = cells_x // devices
    state = pltpu.VMEM((2, cells_x + 16, LANES), F32)
    (both,) = call(
        slide_kernel,
        [],
        strips,
        [(devices, 2, own_rows, LANES)],
        [state, state] + [pltpu.VMEM((cells_x + 16, LANES), F32)] * 2,
        fetch=True,
    )
    both = lax.all_to_all(
        both[..., :w], ("sec", "gx", "gy"), split_axis=0, concat_axis=0, tiled=True
    )

    one = (tiles, total, LANES)
    stage_count = 1 if w == LANES else n
    results = call(
        functools.partial(wave_kernel, n, w, cells_x, nb * tile_y),
        [],
        [wide, edge_u, got_a, got_b, slide_from_low, slide_from_high, *blocks],
        [(w, tile_x)] * n + [(4, tiles - 1, tile_x, LANES)],
        [
            pltpu.VMEM(shape, F32)
            for shape in (
                one,
                (LAYERS, *one),
                (LAYERS, *one),
                (LAYERS, *one),
                (LAYERS, *one),
                (5, *one),
                one,
                (2, *one),
                (2, *one),
                one,
                one,
                one,
                (tiles - 1, total, LANES),
                (n, w, tile_x),
                (stage_count, rows, LANES),
                halo,
                halo,
            )
        ],
        flops=10**9,
        moved=10**7,
        room=30,
    )
    loads, fields = results[:n], results[n]
    parts = [loads[0]] + [across(loads[s], s) for s in range(1, n)]
    surface_out, pressure_out = call(
        turn_kernel, [], [fields], [(tile_y, tile_x), (LAYERS, tile_y, tile_x)]
    )
    if w % LANES == 0:
        last_h, last_m = call(
            functools.partial(place_slide_kernel, secs, n, gys),
            [],
            [both],
            [(own_rows, devices * w)] * 2,
        )
    else:
        both = both.reshape(secs, n, gys, 2, own_rows, w)
        last_h, last_m = jnp.transpose(both, (3, 4, 0, 2, 1, 5)).reshape(2, own_rows, -1)
    parts, last_h, last_m, surface_out = lax.optimization_barrier((parts, last_h, last_m, surface_out))
    (bottom,) = call(functools.partial(place_load_kernel, n), [], parts, [(w, cells_x)])
    return (surface_out, pressure_out, bottom[None, None], last_h, last_m)


def solution(mesh):
    strip = P(("sec", "gy"), "gx", None, None)
    tile = P(("sec", "gy"), "gx")
    layered = P(None, ("sec", "gy"), "gx")
    return jax.shard_map(
        shards,
        mesh=mesh,
        in_specs=(strip, strip, strip, strip, tile, layered, layered, tile, P()),
        out_specs=(
            tile,
            layered,
            strip,
            P(("sec", "gx", "gy"), None),
            P(("sec", "gx", "gy"), None),
        ),
        check_vma=False,
    )
```
